128 devices in a mesh: group: 8 (over y, core), member: 16 (over z, x).
Axes of the slice: x: 4, y: 4, z: 4, core: 2. Of those that a mesh axis runs over, the one named last changes fastest.
Arguments:
- volume_frac: float32 [512, 1024, 256], P('group', 'member'), may hold values from 0 to 1
- velocity: bfloat16 [3, 512, 1024, 256], P(None, 'group', 'member'), may hold values from -6 to 6
- drop_block: int32 [8, 16, 16], P('group', 'member'), may hold values from 0 to 255, as said below
- drop_owner: int32 [8, 16, 16, 1], P('group', 'member'), may hold values from 0 to 15; in each aligned block of 16 rows (0 to 15, 16 to 31, ..., all dimensions but the last counted through in order) at most 2 rows name the same one
- parcel_vel: float32 [8, 16, 16, 2, 3, 512], P('group', 'member'), may hold values from -6 to 6
- parcel_rate: float32 [8, 16, 16, 2, 512], P('group', 'member'), may hold values from 0.05 to 0.8
- parcel_weight: float32 [8, 16, 16, 2, 512], P('group', 'member'), may hold values from 0.3 to 3
- parcel_cell: int32 [8, 16, 16, 2, 512], P('group', 'member'), may hold values from 0 to 4095
Outputs:
- frac_next: float32 [512, 1024, 256], P('group', 'member')
- velocity_next: bfloat16 [3, 512, 1024, 256], P(None, 'group', 'member')
- parcel_next: float32 [8, 16, 16, 2, 3, 512], P('group', 'member')
The draws below stay inside these ranges and needn't reach their ends.
Inputs may be any that keep to these rules, and one draw needn't show every extreme that they name: `drop_block`: the 16 entries of one device are distinct. `drop_owner`: no owner gets more than 2 of one device's droplet blocks; some device sends exactly 2 to one owner.
All inputs are finite; a program needn't handle non-finite values.
Results may differ from the reference program's by a relative error of at most 0.001.
Values may be sent and summed in bfloat16 or wider, within the bound.
A program may use at most 448 MiB of HBM per device.

```python
import math
import jax
import jax.numpy as jnp
import numpy as np
from jax import lax

CX = 64
CY = 64
CZ = 256
DROP_DEV = 16
CAP = 2
PT = 512
NB_DEV = 256
NX = 512
NY = 1024
N_GROUP = 8
N_MEMBER = 16


def draw_drop_block(key, part):
    keys = jax.random.split(key, N_GROUP * N_MEMBER)
    chosen = jax.vmap(lambda one_key: jax.random.permutation(one_key, NB_DEV)[:DROP_DEV])(keys)
    return chosen.reshape(N_GROUP, N_MEMBER, DROP_DEV).astype(jnp.int32)


def with_ends(drawn, rng, least, largest):
    extent = drawn.shape
    spot = [jax.random.randint(jax.random.fold_in(rng, axis), (), 0, extent[axis]) for axis in range(len(extent))]
    drawn = drawn.at[tuple(spot)].set(least)
    longest = extent.index(max(extent))
    spot[longest] = (spot[longest] + 1) % extent[longest]
    return drawn.at[tuple(spot)].set(largest)


def level_of(stream_key, extent, cuts, low, largest):
    def one(position, parts):
        heights = jax.random.uniform(jax.random.fold_in(jax.random.fold_in(stream_key, 6), position), (parts,), jnp.float32, low / len(cuts), largest / len(cuts))
        return jnp.repeat(jnp.exp(heights), extent[position] // parts).reshape((-1,) + (1,) * (len(extent) - position - 1))

    loudness = one(*cuts[0])
    for cut in cuts[1:]:
        loudness = loudness * one(*cut)
    return loudness


def deal_out(stream_key, own, number, rows, amount, top, limit, lean):
    ranking = jax.random.permutation(stream_key, amount)
    heavy_load, usual = load_shares(amount, rows * top, limit, lean, True), load_shares(amount, rows * top, limit, lean, False)
    places = jnp.arange(amount)

    def named(sizes, rotation):
        used = int((sizes > 0).sum())
        fixed = max(1, used // 4)
        passed = fixed + (places - fixed + rotation * (used - fixed)) % max(1, amount - fixed)
        return jnp.zeros((amount,), jnp.int32).at[ranking[jnp.where(places < fixed, places, passed)]].set(jnp.asarray(sizes, jnp.int32))

    sizes = jnp.where(number % 4 == 0, named(heavy_load, number // 4), named(usual, number - number // 4 - 1))
    mixed = jax.random.permutation(jax.random.fold_in(own, 3), amount)
    donor, receiver = mixed[0:amount // 2 * 2:2], mixed[1:amount // 2 * 2:2]
    room = jnp.minimum(sizes[donor] - 1, limit - sizes[receiver]) // 2
    room = jnp.where((donor == ranking[0]) | (receiver == ranking[0]) | (sizes[receiver] == 0), 0, jnp.maximum(room, 0))
    passed = jax.random.randint(jax.random.fold_in(own, 4), (amount // 2,), 0, 1 << 20) % (room + 1)
    sizes = sizes.at[donor].add(-passed).at[receiver].add(passed)
    members = jnp.searchsorted(jnp.cumsum(sizes), jnp.arange(rows * top), side="right").astype(jnp.int32)
    table = members.reshape(top, rows).T
    table = table[jax.random.permutation(jax.random.fold_in(own, 1), rows)]
    rotation = jax.random.randint(jax.random.fold_in(own, 2), (rows, 1), 0, top)
    return jnp.take_along_axis(table, (jnp.arange(top)[None, :] + rotation) % top, axis=1)


def load_shares(amount, total, bound, lean, full):
    loads = [(1 << 20) // math.isqrt(standing ** lean) + 1 for standing in range(1, amount + 1)]
    largest = bound if full else min(bound, max(-(-total // amount), total * loads[0] // sum(loads)))
    least = 1 if total - largest >= amount - 1 else 0
    holding, rest = [largest] + [least] * (amount - 1), total - largest - least * (amount - 1)
    while rest > 0:
        movable = [i for i in range(1, amount) if holding[i] < largest] or [i for i in range(1, amount) if holding[i] < bound]
        mass, left = sum([loads[i] for i in movable]), rest
        for i in movable:
            addition = min(bound - holding[i], max(1, left * loads[i] // mass), rest)
            holding[i] = holding[i] + addition
            rest = rest - addition
    return np.array(holding)


def gaussian(key, extent, width, limit, shards=(), kind=jnp.bfloat16):
    result = width * jax.random.normal(key, extent, jnp.float32)
    if shards:
        result = result * level_of(key, extent, shards, -0.22, 0.18)
    return jnp.clip(result, -limit, limit).astype(kind)


def setup_inputs(seed: int = 0) -> dict:
    streams_of = jax.random.split(jax.random.key(seed), 9)
    volume_frac = jnp.clip(1.0 * jax.random.uniform(streams_of[0], (NX, NY, CZ), jnp.float32) ** level_of(streams_of[0], (NX, NY, CZ), ((0, 8), (1, 16)), -0.2, 0.2), 0.0, 1.0)
    velocity = gaussian(streams_of[1], (3, NX, NY, CZ), 1.0, 6.0, ((1, 8), (2, 16)))
    drop_block = draw_drop_block(jax.random.fold_in(streams_of[8], 71), 0)
    drop_owner_keys = jax.random.split(jax.random.fold_in(streams_of[3], 1), N_GROUP * N_MEMBER * DROP_DEV // DROP_DEV)
    drop_owner_turns = jax.random.permutation(jax.random.fold_in(streams_of[3], 3), N_GROUP * N_MEMBER * DROP_DEV // DROP_DEV)
    drop_owner = jax.vmap(lambda own, number: deal_out(jax.random.fold_in(streams_of[3], 2), own, number, DROP_DEV, N_MEMBER, 1, CAP, 2))(drop_owner_keys, drop_owner_turns).reshape((N_GROUP, N_MEMBER, DROP_DEV, 1))
    parcel_vel = gaussian(streams_of[4], (N_GROUP, N_MEMBER, N_MEMBER, CAP, 3, PT), 1.0, 6.0, ((0, 8), (1, 16)), jnp.float32)
    parcel_rate = jnp.clip(jnp.exp(math.log(0.8) - 2.7725887 * jax.random.uniform(streams_of[5], (N_GROUP, N_MEMBER, N_MEMBER, CAP, PT), jnp.float32) ** level_of(streams_of[5], (N_GROUP, N_MEMBER, N_MEMBER, CAP, PT), ((0, 8), (1, 16)), -0.2, 0.2)), 0.05, 0.8)
    parcel_weight = jnp.clip(jnp.exp(math.log(3.0) - 2.3025851 * jax.random.uniform(streams_of[6], (N_GROUP, N_MEMBER, N_MEMBER, CAP, PT), jnp.float32) ** level_of(streams_of[6], (N_GROUP, N_MEMBER, N_MEMBER, CAP, PT), ((0, 8), (1, 16)), -0.2, 0.2)), 0.3, 3.0)
    parcel_cell = with_ends(jax.random.randint(streams_of[7], (N_GROUP, N_MEMBER, N_MEMBER, CAP, PT), 0, 4096), jax.random.fold_in(streams_of[7], 1), 0, 4095).astype(jnp.int32)
    return {"volume_frac": volume_frac, "velocity": velocity, "drop_block": drop_block, "drop_owner": drop_owner, "parcel_vel": parcel_vel, "parcel_rate": parcel_rate, "parcel_weight": parcel_weight, "parcel_cell": parcel_cell}


courant = 0.025


def face_div(frac_pad, speed_pad, along):
    inner = [slice(1, -1)] * 3
    lower_cut = list(inner)
    lower_cut[along] = slice(0, -1)
    upper_cut = list(inner)
    upper_cut[along] = slice(1, None)
    left_frac = frac_pad[tuple(lower_cut)]
    right_frac = frac_pad[tuple(upper_cut)]
    left_speed = speed_pad[tuple(lower_cut)]
    face_flux = courant * (jnp.maximum(left_speed, 0.0) * left_frac + jnp.minimum(left_speed, 0.0) * right_frac)
    length = face_flux.shape[along]
    return lax.slice_in_dim(face_flux, 1, length, axis=along) - lax.slice_in_dim(face_flux, 0, length - 1, axis=along)


def drag_one(block_data, parcel_v, drag_rate, weight, cell_ids):
    sampled = block_data[:, cell_ids].astype(jnp.float32)
    gas_share = 1.0 - sampled[3]
    acceleration = drag_rate * gas_share * (sampled[:3] - parcel_v)
    deposit_w = (weight * acceleration).astype(jnp.bfloat16)
    source = jnp.zeros((3, 4096), jnp.float32).at[:, cell_ids].add(deposit_w.astype(jnp.float32))
    return parcel_v + acceleration, source.astype(jnp.bfloat16)


def reference(volume_frac, velocity, drop_block, drop_owner, parcel_vel, parcel_rate, parcel_weight, parcel_cell):
    frac_pad = jnp.pad(volume_frac, 1)
    speed_pad = jnp.pad(velocity.astype(jnp.float32), ((0, 0), (1, 1), (1, 1), (1, 1)))
    change = face_div(frac_pad, speed_pad[0], 0) + face_div(frac_pad, speed_pad[1], 1) + face_div(frac_pad, speed_pad[2], 2)
    frac_next = jnp.minimum(volume_frac - change, 1.0)
    owners = drop_owner[..., 0]
    positions = jnp.arange(DROP_DEV, dtype=jnp.int32)
    earlier = positions[:, None] < positions[None, :]
    places = jnp.sum(((owners[..., :, None] == owners[..., None, :]) & earlier).astype(jnp.int32), axis=-2).astype(jnp.int32)

    def per_group(group_idx):
        frac_slab = lax.dynamic_slice_in_dim(volume_frac, group_idx * CX, CX, 0)
        vel_slab = lax.dynamic_slice_in_dim(velocity, group_idx * CX, CX, 1)
        combined = jnp.concatenate([vel_slab, frac_slab[None].astype(jnp.bfloat16)], 0)
        blocks = combined.reshape(4, CX // 16, 16, N_MEMBER, CY // 16, 16, CZ // 16, 16)
        blocks = blocks.transpose(3, 1, 4, 6, 0, 2, 5, 7).reshape(N_MEMBER, NB_DEV, 4, 4096)
        block_ids = drop_block[group_idx]
        picked = jnp.take_along_axis(blocks, block_ids[:, :, None, None], axis=1)
        owner_row = owners[group_idx]
        place_row = places[group_idx]
        source_row = jnp.broadcast_to(jnp.arange(N_MEMBER, dtype=jnp.int32)[:, None], owner_row.shape)
        got_vel = parcel_vel[group_idx][owner_row, source_row, place_row]
        got_rate = parcel_rate[group_idx][owner_row, source_row, place_row]
        got_weight = parcel_weight[group_idx][owner_row, source_row, place_row]
        got_cell = parcel_cell[group_idx][owner_row, source_row, place_row]
        new_vel, source = jax.vmap(jax.vmap(drag_one))(picked, got_vel, got_rate, got_weight, got_cell)
        vel_out = parcel_vel[group_idx].at[owner_row, source_row, place_row].set(new_vel)
        deposit = jnp.zeros((N_MEMBER, NB_DEV, 3, 4096), jnp.float32).at[source_row, block_ids].add(source.astype(jnp.float32))
        deposit = deposit.reshape(N_MEMBER, CX // 16, CY // 16, CZ // 16, 3, 16, 16, 16)
        drag_field = deposit.transpose(4, 1, 5, 0, 2, 6, 3, 7).reshape(3, CX, NY, CZ)
        return vel_out, drag_field

    parcel_next, drag_field = lax.map(per_group, jnp.arange(N_GROUP, dtype=jnp.int32))
    drag_field = drag_field.transpose(1, 0, 2, 3, 4).reshape(3, NX, NY, CZ)
    velocity_next = (velocity.astype(jnp.float32) + drag_field).astype(jnp.bfloat16)
    return (frac_next, velocity_next, parcel_next)
```

```python
import functools

import jax
import jax.numpy as jnp
from jax import lax
from jax.experimental import pallas as pl
from jax.experimental.pallas import tpu as pltpu
from jax.sharding import PartitionSpec as P

CAP = 2
COURANT = 0.025
MESH = pl.DeviceIdType.MESH
F32 = jnp.float32
BF16 = jnp.bfloat16


def corner(block_id, blocks_y, blocks_z):
    first = lax.div(block_id, blocks_y * blocks_z)
    second = lax.rem(lax.div(block_id, blocks_z), blocks_y)
    third = lax.rem(block_id, blocks_z)
    return first, second, third


def cell_parts(cell):
    row = jnp.floor(cell * (1.0 / 16.0))
    return row, cell - 16.0 * row


def hot_rows(row):
    parcels = row.shape[-1]
    ids = lax.broadcasted_iota(jnp.int32, (256, parcels), 0).astype(F32)
    return jnp.where(ids == row, 1.0, 0.0).astype(BF16)


def hot_depth(depth):
    parcels = depth.shape[-1]
    ids = lax.broadcasted_iota(jnp.int32, (16, parcels), 0).astype(F32)
    return jnp.where(ids == depth, 1.0, 0.0)


def exchange_kernel(
    groups,
    members,
    block_hbm,
    owner_hbm,
    vel_hbm,
    frac_hbm,
    pv_hbm,
    pr_hbm,
    pw_hbm,
    pc_hbm,
    vel_v,
    next_v,
    source_ref,
    back_ref,
    frac_v,
    pv_v,
    pr_v,
    pw_v,
    pc_v,
    pack_v,
    got_v,
    block_v,
    samp_v,
    give_v,
    fluxx_v,
    hxu_v,
    hxf_v,
    hxn_v,
    hyu_v,
    hyf_v,
    hyn_v,
    syu_v,
    syf_v,
    syn_v,
    block_s,
    owner_s,
    place_s,
    slot_s,
    name_sem,
    parcel_sem,
    load_sem,
    send_sem,
    recv_sem,
    back_send,
    back_recv,
    face_send,
    face_recv,
):
    group = lax.axis_index("group")
    member = lax.axis_index("member")
    drops = owner_hbm.shape[0]
    blocks_x, _, blocks_y, _, depth = frac_hbm.shape
    parcels = pv_hbm.shape[-1]
    blocks_z = depth // 16

    parcel_loads = [
        pltpu.make_async_copy(src, dst, parcel_sem.at[i])
        for i, (src, dst) in enumerate(
            [(pv_hbm, pv_v), (pr_hbm, pr_v), (pw_hbm, pw_v), (pc_hbm, pc_v)]
        )
    ]
    loads = []
    for c in range(blocks_x):
        loads.append(
            (
                pltpu.make_async_copy(frac_hbm.at[c], frac_v.at[c], load_sem.at[0, c]),
                pltpu.make_async_copy(vel_hbm.at[:, c], vel_v.at[:, c], load_sem.at[1, c]),
            )
        )
    names = [
        pltpu.make_async_copy(block_hbm, block_s, name_sem.at[0]),
        pltpu.make_async_copy(owner_hbm, owner_s, name_sem.at[1]),
    ]
    for copy in names + parcel_loads:
        copy.start()
    for pair in loads:
        for copy in pair:
            copy.start()

    up = lax.rem(group + 1, groups)
    down = lax.rem(group + groups - 1, groups)
    right = lax.rem(member + 1, members)
    left = lax.rem(member + members - 1, members)
    barrier = pltpu.get_barrier_semaphore()
    for i in range(1, members):
        peer = lax.rem(member + i, members)
        pl.semaphore_signal(barrier, inc=1, device_id=(group, peer), device_id_type=MESH)
    for near in (up, down):
        pl.semaphore_signal(barrier, inc=1, device_id=(near, member), device_id_type=MESH)

    for copy in names:
        copy.wait()
    owners = [owner_s[j] for j in range(drops)]
    slots = []
    for j in range(drops):
        place = jnp.int32(0)
        for i in range(j):
            place = place + jnp.where(owners[i] == owners[j], 1, 0)
        place_s[j] = place
        slots.append(owners[j] * CAP + place)
    for s in range(members * CAP):
        found = jnp.int32(drops)
        for j in range(drops):
            found = jnp.where(slots[j] == s, j, found)
        slot_s[s] = found

    for copy in parcel_loads:
        copy.wait()
    pack_v[:, 0:3] = pv_v[...]
    pack_v[:, 3] = pr_v[...] * pw_v[...]
    pack_v[:, 4] = pc_v[...].astype(F32)

    pl.semaphore_wait(barrier, members + 1)

    sends = []
    for i in range(1, members):
        peer = lax.rem(member + i, members)
        copy = pltpu.make_async_remote_copy(
            src_ref=pack_v.at[peer],
            dst_ref=got_v.at[member],
            send_sem=send_sem.at[i],
            recv_sem=recv_sem.at[i],
            device_id=(group, peer),
            device_id_type=MESH,
        )
        copy.start()
        sends.append(copy)
    got_v[member] = pack_v[member]

    def face(src, dst, number, device):
        copy = pltpu.make_async_remote_copy(
            src_ref=src,
            dst_ref=dst,
            send_sem=face_send.at[number],
            recv_sem=face_recv.at[number],
            device_id=device,
            device_id_type=MESH,
        )
        copy.start()
        return copy

    faces = [
        face(vel_hbm.at[0, blocks_x - 1, 15], hxu_v, 0, (up, member)),
        face(frac_hbm.at[blocks_x - 1, 15], hxf_v, 1, (up, member)),
        face(frac_hbm.at[0, 0], hxn_v, 2, (down, member)),
    ]

    for c in range(blocks_x):
        for copy in loads[c]:
            copy.wait()

        def edge(x, carry):
            syf_v[c, x] = frac_v[c, x, blocks_y - 1, 15:16, :]
            syn_v[c, x] = frac_v[c, x, 0, 0:1, :]
            syu_v[c, x] = vel_v[1, c, x, blocks_y - 1].astype(F32)[15:16]
            return carry

        lax.fori_loop(0, 16, edge, 0, unroll=8)
    faces += [
        face(syu_v, hyu_v, 3, (group, right)),
        face(syf_v, hyf_v, 4, (group, right)),
        face(syn_v, hyn_v, 5, (group, left)),
    ]

    column = lax.broadcasted_iota(jnp.int32, (64, depth), 0)
    lane = lax.broadcasted_iota(jnp.int32, (64, depth), 1)

    def extract(j, carry):
        bx, by, bz = corner(block_s[j], blocks_y, blocks_z)
        wanted = lane - bz * 16
        total = jnp.zeros((64, 256), F32)
        for k in range(4):
            if k < 3:
                part = vel_v[k, bx, :, by]
            else:
                part = frac_v[bx, :, by].astype(BF16)
            part = part.reshape(256, depth)
            pick = jnp.where(wanted == column - 16 * k, 1.0, 0.0)
            pick = jnp.where(column // 16 == k, pick, 0.0).astype(BF16)
            total = total + lax.dot_general(
                pick, part, (((1,), (1,)), ((), ())), preferred_element_type=F32
            )
        block_v[j] = total.astype(BF16)
        return carry

    lax.fori_loop(0, drops, extract, 0, unroll=4)

    for i in range(1, members):
        peer = lax.rem(member + members - i, members)
        pltpu.make_async_remote_copy(
            src_ref=pack_v.at[peer],
            dst_ref=got_v.at[peer],
            send_sem=send_sem.at[i],
            recv_sem=recv_sem.at[i],
            device_id=(group, peer),
            device_id_type=MESH,
        ).wait_recv()

    def pair_row(j, q):
        both = got_v[owner_s[j], q]
        return jnp.where(place_s[j] == 0, both[0:1], both[1:2])

    def sample(j, carry):
        row, deep = cell_parts(pair_row(j, 4))
        picked = jnp.dot(block_v[j], hot_rows(row), preferred_element_type=F32)
        hot = hot_depth(deep)
        for q in range(4):
            samp_v[j, q : q + 1] = jnp.sum(
                picked[16 * q : 16 * q + 16] * hot, axis=0, keepdims=True
            )
        return carry

    lax.fori_loop(0, drops, sample, 0, unroll=4)
    samp_v[drops, 0:3] = jnp.zeros((3, parcels), F32)
    samp_v[drops, 3:4] = jnp.ones((1, parcels), F32)

    def give(s, carry):
        give_v[s // CAP, s % CAP] = samp_v[slot_s[s]].astype(BF16)
        return carry

    lax.fori_loop(0, members * CAP, give, 0, unroll=8)
    for i in range(1, members):
        peer = lax.rem(member + i, members)
        copy = pltpu.make_async_remote_copy(
            src_ref=give_v.at[peer],
            dst_ref=back_ref.at[member],
            send_sem=back_send.at[i],
            recv_sem=back_recv.at[i],
            device_id=(group, peer),
            device_id_type=MESH,
        )
        copy.start()
        sends.append(copy)
    back_ref[member] = give_v[member]

    def scatter(j, carry):
        row, deep = cell_parts(pair_row(j, 4))
        hot = hot_depth(deep)
        pull = pair_row(j, 3) * (1.0 - samp_v[j, 3:4])
        parts = []
        for q in range(3):
            drag = pull * (samp_v[j, q : q + 1] - pair_row(j, q))
            parts.append((drag.astype(BF16).astype(F32) * hot).astype(BF16))
        spread = jnp.concatenate(parts, axis=0)
        source = lax.dot_general(
            hot_rows(row), spread, (((1,), (1,)), ((), ())), preferred_element_type=F32
        )
        source_ref[j] = source.astype(BF16)
        return carry

    lax.fori_loop(0, drops, scatter, 0, unroll=4)

    for copy in faces:
        copy.wait()
    low_x = jnp.where(group > 0, 1.0, 0.0)
    high_x = jnp.where(group < groups - 1, 1.0, 0.0)
    low_y = jnp.where(member > 0, 1.0, 0.0)
    high_y = jnp.where(member < members - 1, 1.0, 0.0)
    frac_v[blocks_x, 0] = hxn_v[...] * high_x

    def flux(speed, here, there):
        return speed * jnp.where(speed > 0.0, here, there)

    fluxx_v[...] = flux(hxu_v[...].astype(F32) * low_x, hxf_v[...], frac_v[0, 0])

    def full(row):
        return jnp.broadcast_to(row, (8, 128))

    row_id = lax.broadcasted_iota(jnp.int32, (8, 128), 0)
    lane_id = lax.broadcasted_iota(jnp.int32, (8, 128), 1)
    first_row, last_row = row_id == 0, row_id == 7
    first_lane, last_lane = lane_id == 0, lane_id == 127
    halves = [slice(h * 128, h * 128 + 128) for h in range(depth // 128)]
    tiles = blocks_y * 2

    def split(row):
        return [full(row[:, h]) for h in halves]

    def one_plane(bx, x):
        def at(t):
            return t // 2, slice(8 * (t % 2), 8 * (t % 2) + 8)

        def speeds(k, t):
            pairs = [vel_v[k, bx, x, t, :, h].astype(F32) for h in halves]
            return [[p[8 * i : 8 * i + 8] for p in pairs] for i in range(2)]

        after = bx * 16 + x + 1
        bn, xn = lax.div(after, 16), lax.rem(after, 16)
        here = [[frac_v[(bx, x) + at(t) + (h,)] for h in halves] for t in range(tiles)]
        behind = split(flux(hyu_v[bx, x] * low_y, hyf_v[bx, x], frac_v[bx, x, 0, 0:1, :]))
        beyond = split(hyn_v[bx, x] * high_y)
        rolled = [pltpu.roll(f, 7, 0) for f in here[0]]
        for t in range(tiles):
            if t % 2 == 0:
                pair = [speeds(k, t // 2) for k in range(3)]
            speed = [pair[k][t % 2] for k in range(3)]
            if t + 1 < tiles:
                rolled_next = [pltpu.roll(f, 7, 0) for f in here[t + 1]]
            else:
                rolled_next = beyond
            lanes = [pltpu.roll(f, 127, 1) for f in here[t]] + [jnp.zeros((8, 128), F32)]
            deep = [
                flux(speed[2][i], here[t][i], jnp.where(last_lane, lanes[i + 1], lanes[i]))
                for i in range(len(halves))
            ]
            turned = [jnp.zeros((8, 128), F32)] + [pltpu.roll(d, 1, 1) for d in deep]
            for i, h in enumerate(halves):
                spot = at(t) + (h,)
                now = flux(speed[0][i], here[t][i], frac_v[(bn, xn) + spot])
                change = now - fluxx_v[spot]
                fluxx_v[spot] = now
                ahead = jnp.where(last_row, rolled_next[i], rolled[i])
                now = flux(speed[1][i], here[t][i], ahead)
                moved = pltpu.roll(now, 1, 0)
                change = change + (now - jnp.where(first_row, behind[i], moved))
                behind[i] = moved
                under = jnp.where(first_lane, turned[i], turned[i + 1])
                change = change + (deep[i] - under)
                next_v[(bx, x) + spot] = jnp.minimum(here[t][i] - COURANT * change, 1.0)
            rolled = rolled_next

    def plane(n, carry):
        bx, x = lax.div(n, 4), lax.rem(n, 4) * 4
        for i in range(4):
            one_plane(bx, x + i)
        return carry

    lax.fori_loop(0, blocks_x * 4, plane, 0)

    for i in range(1, members):
        peer = lax.rem(member + members - i, members)
        pltpu.make_async_remote_copy(
            src_ref=give_v.at[peer],
            dst_ref=back_ref.at[peer],
            send_sem=back_send.at[i],
            recv_sem=back_recv.at[i],
            device_id=(group, peer),
            device_id_type=MESH,
        ).wait_recv()
    for copy in sends:
        copy.wait_send()


def field_kernel(
    block_s,
    vel_ref,
    next_ref,
    source_ref,
    back_ref,
    pv_ref,
    pr_ref,
    frac_out,
    vel_out,
    pv_out,
    fresh_v,
    lead_s,
    store_sem,
    block_sem,
):
    drops = block_s.shape[0]
    members = back_ref.shape[0]
    _, blocks_x, _, blocks_y, _, depth = vel_ref.shape
    blocks_z = depth // 16
    bulk = [
        pltpu.make_async_copy(vel_ref.at[:, c], vel_out.at[:, c], store_sem.at[c])
        for c in range(blocks_x)
    ]
    frac_copy = pltpu.make_async_copy(next_ref, frac_out, store_sem.at[blocks_x])
    for copy in bulk + [frac_copy]:
        copy.start()

    keys = [lax.div(block_s[j], 8) for j in range(drops)]
    for j in range(drops):
        lead = jnp.int32(j)
        for i in reversed(range(j)):
            lead = jnp.where(keys[i] == keys[j], i, lead)
        lead_s[j] = lead

    def spot(j):
        bx, by, bz = corner(block_s[j], blocks_y, blocks_z)
        z0 = pl.multiple_of(lax.div(bz, 8) * 128, 128)
        return bx, by, pl.ds(z0, 128), lax.rem(bz, 8) * 16

    def begin(j, carry):
        bx, by, lanes, _ = spot(j)
        for k in range(3):
            fresh_v[j, k] = vel_ref[k, bx, :, by, :, lanes]
        return carry

    lax.fori_loop(0, drops, begin, 0, unroll=4)

    lane = lax.broadcasted_iota(jnp.int32, (48, 128), 1)
    column = lax.broadcasted_iota(jnp.int32, (48, 128), 0)

    def patch(j, carry):
        _, _, _, shift = spot(j)
        wanted = lane - shift
        source = source_ref[j]
        lead = lead_s[j]
        for k in range(3):
            pick = jnp.where(wanted == column - 16 * k, 1.0, 0.0)
            pick = jnp.where(column // 16 == k, pick, 0.0).astype(BF16)
            moved = jnp.dot(source, pick, preferred_element_type=F32)
            old = fresh_v[lead, k].astype(F32).reshape(256, 128)
            fresh_v[lead, k] = (old + moved).astype(BF16).reshape(16, 16, 128)
        return carry

    lax.fori_loop(0, drops, patch, 0, unroll=4)

    def block_copy(j):
        bx, by, lanes, _ = spot(j)
        return pltpu.make_async_copy(
            fresh_v.at[j], vel_out.at[:, bx, :, by, :, lanes], block_sem.at[j]
        )

    for copy in bulk:
        copy.wait()
    for j in range(drops):

        @pl.when(lead_s[j] == j)
        def _():
            block_copy(j).start()

    def gain_pair(owner, carry):
        sampled = [back_ref[owner, place].astype(F32) for place in range(CAP)]
        rate = pr_ref[owner]
        old = pv_ref[owner]
        share = jnp.concatenate([s[3:4] for s in sampled], axis=0)
        pull = rate * (1.0 - share)
        for q in range(3):
            speed = jnp.concatenate([s[q : q + 1] for s in sampled], axis=0)
            pv_out[owner, q] = old[q] + pull * (speed - old[q])
        return carry

    lax.fori_loop(0, members, gain_pair, 0, unroll=4)
    frac_copy.wait()
    for j in range(drops):

        @pl.when(lead_s[j] == j)
        def _():
            block_copy(j).wait()


def solution(mesh):
    groups, members = mesh.shape["group"], mesh.shape["member"]

    def per_device(
        volume_frac,
        velocity,
        drop_block,
        drop_owner,
        parcel_vel,
        parcel_rate,
        parcel_weight,
        parcel_cell,
    ):
        planes, rows, depth = volume_frac.shape
        parcels = parcel_vel.shape[-1]
        drops = drop_block.shape[-1]
        block_ids = drop_block.reshape(drops)
        owners = drop_owner.reshape(drops)
        pv = parcel_vel[0, 0].transpose(0, 2, 1, 3)
        pr, pw, pc = parcel_rate[0, 0], parcel_weight[0, 0], parcel_cell[0, 0]
        smem = pl.BlockSpec(memory_space=pltpu.SMEM)
        vmem = pl.BlockSpec(memory_space=pltpu.VMEM)
        hbm = pl.BlockSpec(memory_space=pltpu.HBM)
        shaped = jax.ShapeDtypeStruct
        blocks_x, blocks_y = planes // 16, rows // 16
        vel6 = velocity.reshape(3, blocks_x, 16, blocks_y, 16, depth)
        frac5 = volume_frac.reshape(blocks_x, 16, blocks_y, 16, depth)
        face_x = (blocks_y, 16, depth)
        face_y = (blocks_x, 16, 1, depth)
        inputs = [
            pltpu.with_memory_space_constraint(a, pltpu.HBM)
            for a in (block_ids, owners, vel6, frac5, pv, pr, pw, pc)
        ]
        vel_now, frac_next, source, back = pl.pallas_call(
            functools.partial(exchange_kernel, groups, members),
            out_shape=(
                shaped(vel6.shape, BF16),
                shaped(frac5.shape, F32),
                shaped((drops, 256, 48), BF16),
                shaped((members, CAP, 4, parcels), BF16),
            ),
            in_specs=[hbm] * 8,
            out_specs=(vmem,) * 4,
            scratch_shapes=[
                pltpu.VMEM((blocks_x + 1, 16, blocks_y, 16, depth), F32),
                pltpu.VMEM(pv.shape, F32),
                pltpu.VMEM(pr.shape, F32),
                pltpu.VMEM(pw.shape, F32),
                pltpu.VMEM(pc.shape, jnp.int32),
                pltpu.VMEM((members, 5, CAP, parcels), F32),
                pltpu.VMEM((members, 5, CAP, parcels), F32),
                pltpu.VMEM((drops, 64, 256), BF16),
                pltpu.VMEM((drops + 1, 4, parcels), F32),
                pltpu.VMEM((members, CAP, 4, parcels), BF16),
                pltpu.VMEM(face_x, F32),
                pltpu.VMEM(face_x, BF16),
                pltpu.VMEM(face_x, F32),
                pltpu.VMEM(face_x, F32),
                pltpu.VMEM(face_y, F32),
                pltpu.VMEM(face_y, F32),
                pltpu.VMEM(face_y, F32),
                pltpu.VMEM(face_y, F32),
                pltpu.VMEM(face_y, F32),
                pltpu.VMEM(face_y, F32),
                pltpu.SMEM((drops,), jnp.int32),
                pltpu.SMEM((drops,), jnp.int32),
                pltpu.SMEM((drops,), jnp.int32),
                pltpu.SMEM((members * CAP,), jnp.int32),
                pltpu.SemaphoreType.DMA((2,)),
                pltpu.SemaphoreType.DMA((4,)),
                pltpu.SemaphoreType.DMA((2, blocks_x)),
                pltpu.SemaphoreType.DMA((members,)),
                pltpu.SemaphoreType.DMA((members,)),
                pltpu.SemaphoreType.DMA((members,)),
                pltpu.SemaphoreType.DMA((members,)),
                pltpu.SemaphoreType.DMA((6,)),
                pltpu.SemaphoreType.DMA((6,)),
            ],
            compiler_params=pltpu.CompilerParams(
                collective_id=0, has_side_effects=True, vmem_limit_bytes=40 << 20
            ),
            name="exchange",
        )(*inputs)
        frac_next, velocity_next, pv_next = pl.pallas_call(
            field_kernel,
            out_shape=(
                shaped(frac5.shape, F32),
                shaped(vel6.shape, BF16),
                shaped(pv.shape, F32),
            ),
            in_specs=[smem] + [vmem] * 6,
            out_specs=(hbm, hbm, vmem),
            scratch_shapes=[
                pltpu.VMEM((drops, 3, 16, 16, 128), BF16),
                pltpu.SMEM((drops,), jnp.int32),
                pltpu.SemaphoreType.DMA((blocks_x + 1,)),
                pltpu.SemaphoreType.DMA((drops,)),
            ],
            compiler_params=pltpu.CompilerParams(vmem_limit_bytes=40 << 20),
            name="field",
        )(block_ids, vel_now, frac_next, source, back, pv, pr)
        frac_next = frac_next.reshape(volume_frac.shape)
        velocity_next = velocity_next.reshape(velocity.shape)
        parcel_next = pv_next.transpose(0, 2, 1, 3)[None, None]
        return frac_next, velocity_next, parcel_next

    return jax.shard_map(
        per_device,
        mesh=mesh,
        in_specs=(
            P("group", "member", None),
            P(None, "group", "member", None),
            P("group", "member", None),
            P("group", "member", None, None),
            P("group", "member", None, None, None, None),
            P("group", "member", None, None, None),
            P("group", "member", None, None, None),
            P("group", "member", None, None, None),
        ),
        out_specs=(
            P("group", "member", None),
            P(None, "group", "member", None),
            P("group", "member", None, None, None, None),
        ),
        check_vma=False,
    )
```

```python
import functools

import jax
import jax.numpy as jnp
from jax import lax
from jax.experimental import pallas as pl
from jax.experimental.pallas import tpu as pltpu
from jax.sharding import PartitionSpec as P

CAP = 2
COURANT = 0.025
MESH = pl.DeviceIdType.MESH
F32 = jnp.float32
BF16 = jnp.bfloat16


def corner(block_id, blocks_y, blocks_z):
    first = lax.div(block_id, blocks_y * blocks_z)
    second = lax.rem(lax.div(block_id, blocks_z), blocks_y)
    third = lax.rem(block_id, blocks_z)
    return first, second, third


def cell_parts(cell):
    row = jnp.floor(cell * (1.0 / 16.0))
    return row, cell - 16.0 * row


def hot_rows(row):
    parcels = row.shape[-1]
    ids = lax.broadcasted_iota(jnp.int32, (256, parcels), 0).astype(F32)
    return jnp.where(ids == row, 1.0, 0.0).astype(BF16)


def hot_depth(depth):
    parcels = depth.shape[-1]
    ids = lax.broadcasted_iota(jnp.int32, (16, parcels), 0).astype(F32)
    return jnp.where(ids == depth, 1.0, 0.0)


def exchange_kernel(
    groups,
    members,
    block_hbm,
    owner_hbm,
    vel_hbm,
    frac_hbm,
    pv_hbm,
    pr_hbm,
    pw_hbm,
    pc_hbm,
    vel_v,
    next_v,
    source_ref,
    back_ref,
    frac_v,
    pv_v,
    pr_v,
    pw_v,
    pc_v,
    pack_v,
    got_v,
    block_v,
    samp_v,
    give_v,
    fluxx_v,
    hxu_v,
    hxf_v,
    hxn_v,
    hyu_v,
    hyf_v,
    hyn_v,
    syu_v,
    syf_v,
    syn_v,
    block_s,
    owner_s,
    place_s,
    slot_s,
    name_sem,
    parcel_sem,
    load_sem,
    send_sem,
    recv_sem,
    back_send,
    back_recv,
    face_send,
    face_recv,
):
    group = lax.axis_index("group")
    member = lax.axis_index("member")
    drops = owner_hbm.shape[0]
    blocks_x, _, blocks_y, _, depth = frac_hbm.shape
    parcels = pv_hbm.shape[-1]
    blocks_z = depth // 16

    parcel_loads = [
        pltpu.make_async_copy(src, dst, parcel_sem.at[i])
        for i, (src, dst) in enumerate(
            [(pv_hbm, pv_v), (pr_hbm, pr_v), (pw_hbm, pw_v), (pc_hbm, pc_v)]
        )
    ]
    def chunk_loads(c):
        return (
            pltpu.make_async_copy(frac_hbm.at[c], frac_v.at[c], load_sem.at[0, c]),
            pltpu.make_async_copy(vel_hbm.at[:, c], vel_v.at[:, c], load_sem.at[1, c]),
        )

    names = [
        pltpu.make_async_copy(block_hbm, block_s, name_sem.at[0]),
        pltpu.make_async_copy(owner_hbm, owner_s, name_sem.at[1]),
    ]
    for copy in names + parcel_loads:
        copy.start()
    for c in range(blocks_x):
        for copy in chunk_loads(c):
            copy.start()

    up = lax.rem(group + 1, groups)
    down = lax.rem(group + groups - 1, groups)
    right = lax.rem(member + 1, members)
    left = lax.rem(member + members - 1, members)
    barrier = pltpu.get_barrier_semaphore()
    for i in range(1, members):
        peer = lax.rem(member + i, members)
        pl.semaphore_signal(barrier, inc=1, device_id=(group, peer), device_id_type=MESH)
    for near in (up, down):
        pl.semaphore_signal(barrier, inc=1, device_id=(near, member), device_id_type=MESH)

    for copy in names:
        copy.wait()
    owners = [owner_s[j] for j in range(drops)]
    slots = []
    for j in range(drops):
        place = jnp.int32(0)
        for i in range(j):
            place = place + jnp.where(owners[i] == owners[j], 1, 0)
        place_s[j] = place
        slots.append(owners[j] * CAP + place)
    for s in range(members * CAP):
        found = jnp.int32(drops)
        for j in range(drops):
            found = jnp.where(slots[j] == s, j, found)
        slot_s[s] = found

    for copy in parcel_loads:
        copy.wait()
    pack_v[:, 0:3] = pv_v[...]
    pack_v[:, 3] = pr_v[...] * pw_v[...]
    pack_v[:, 4] = pc_v[...].astype(F32)

    low_x = jnp.where(group > 0, 1.0, 0.0)
    high_x = jnp.where(group < groups - 1, 1.0, 0.0)
    low_y = jnp.where(member > 0, 1.0, 0.0)
    high_y = jnp.where(member < members - 1, 1.0, 0.0)

    def flux(speed, here, there):
        return speed * jnp.where(speed > 0.0, here, there)

    row_id = lax.broadcasted_iota(jnp.int32, (8, 128), 0)
    lane_id = lax.broadcasted_iota(jnp.int32, (8, 128), 1)
    first_row, last_row = row_id == 0, row_id == 7
    first_lane, last_lane = lane_id == 0, lane_id == 127
    halves = [slice(h * 128, h * 128 + 128) for h in range(depth // 128)]
    tiles = blocks_y * 2
    nothing = jnp.zeros((8, 128), F32)

    def one_plane(bx, x):
        def at(t):
            return t // 2, slice(8 * (t % 2), 8 * (t % 2) + 8)

        def speeds(k, t):
            pairs = [vel_v[k, bx, x, t, :, h].astype(F32) for h in halves]
            return [[p[8 * i : 8 * i + 8] for p in pairs] for i in range(2)]

        after = bx * 16 + x + 1
        bn, xn = lax.div(after, 16), lax.rem(after, 16)
        here = [[frac_v[(bx, x) + at(t) + (h,)] for h in halves] for t in range(tiles)]
        behind = [nothing] * len(halves)
        rolled = [pltpu.roll(f, 7, 0) for f in here[0]]
        for t in range(tiles):
            if t % 2 == 0:
                pair = [speeds(k, t // 2) for k in range(3)]
            speed = [pair[k][t % 2] for k in range(3)]
            if t + 1 < tiles:
                rolled_next = [pltpu.roll(f, 7, 0) for f in here[t + 1]]
            else:
                rolled_next = [nothing] * len(halves)
            lanes = [pltpu.roll(f, 127, 1) for f in here[t]] + [nothing]
            deep = [
                flux(speed[2][i], here[t][i], jnp.where(last_lane, lanes[i + 1], lanes[i]))
                for i in range(len(halves))
            ]
            turned = [nothing] + [pltpu.roll(d, 1, 1) for d in deep]
            for i, h in enumerate(halves):
                spot = at(t) + (h,)
                now = flux(speed[0][i], here[t][i], frac_v[(bn, xn) + spot])
                change = now - fluxx_v[spot]
                fluxx_v[spot] = now
                ahead = jnp.where(last_row, rolled_next[i], rolled[i])
                now = flux(speed[1][i], here[t][i], ahead)
                moved = pltpu.roll(now, 1, 0)
                change = change + (now - jnp.where(first_row, behind[i], moved))
                behind[i] = moved
                under = jnp.where(first_lane, turned[i], turned[i + 1])
                change = change + (deep[i] - under)
                fresh = here[t][i] - COURANT * change
                capped = jnp.minimum(fresh, 1.0)
                if t == 0:
                    capped = jnp.where(first_row, fresh, capped)
                if t == tiles - 1:
                    capped = jnp.where(last_row, fresh, capped)
                next_v[(bx, x) + spot] = capped
            rolled = rolled_next

    quads = blocks_x * 4

    def quad(n):
        bx, x = lax.div(n, 4), lax.rem(n, 4) * 4
        for i in range(4):
            one_plane(bx, x + i)

    def mend(n, carry):
        bx, x = lax.div(n, 16), lax.rem(n, 16)
        gain = flux(hyu_v[bx, x] * low_y, hyf_v[bx, x], syn_v[bx, x])
        old = next_v[bx, x, 0, 0:1, :]
        next_v[bx, x, 0, 0:1, :] = jnp.minimum(old + COURANT * gain, 1.0)
        loss = jnp.minimum(syu_v[bx, x], 0.0) * (hyn_v[bx, x] * high_y)
        old = next_v[bx, x, blocks_y - 1, 15:16, :]
        next_v[bx, x, blocks_y - 1, 15:16, :] = jnp.minimum(old - COURANT * loss, 1.0)
        return carry

    def edges(c):
        for copy in chunk_loads(c):
            copy.wait()

        def edge(x, carry):
            syf_v[c, x] = frac_v[c, x, blocks_y - 1, 15:16, :]
            syn_v[c, x] = frac_v[c, x, 0, 0:1, :]
            syu_v[c, x] = vel_v[1, c, x, blocks_y - 1].astype(F32)[15:16]
            return carry

        lax.fori_loop(0, 16, edge, 0, unroll=8)

    pl.semaphore_wait(barrier, members + 1)

    sends = []
    for i in range(1, members):
        peer = lax.rem(member + i, members)
        copy = pltpu.make_async_remote_copy(
            src_ref=pack_v.at[peer],
            dst_ref=got_v.at[member],
            send_sem=send_sem.at[i],
            recv_sem=recv_sem.at[i],
            device_id=(group, peer),
            device_id_type=MESH,
        )
        copy.start()
        sends.append(copy)
    got_v[member] = pack_v[member]

    def face(src, dst, number, device):
        copy = pltpu.make_async_remote_copy(
            src_ref=src,
            dst_ref=dst,
            send_sem=face_send.at[number],
            recv_sem=face_recv.at[number],
            device_id=device,
            device_id_type=MESH,
        )
        return copy

    faces = [
        face(vel_hbm.at[0, blocks_x - 1, 15], hxu_v, 0, (up, member)),
        face(frac_hbm.at[blocks_x - 1, 15], hxf_v, 1, (up, member)),
        face(frac_hbm.at[0, 0], hxn_v, 2, (down, member)),
    ]
    for copy in faces:
        copy.start()

    def side_faces():
        return [
            face(syu_v, hyu_v, 3, (group, right)),
            face(syf_v, hyf_v, 4, (group, right)),
            face(syn_v, hyn_v, 5, (group, left)),
        ]

    def drag():
        column = lax.broadcasted_iota(jnp.int32, (64, 128), 0)
        lane = lax.broadcasted_iota(jnp.int32, (64, 128), 1)

        def extract(j, carry):
            bx, by, bz = corner(block_s[j], blocks_y, blocks_z)
            half = lax.div(bz, 8)
            wanted = lane - lax.rem(bz, 8) * 16
            total = jnp.zeros((64, 256), F32)
            for k in range(4):
                if k < 3:
                    part = vel_v[k, bx, :, by]
                else:
                    part = frac_v[bx, :, by].astype(BF16)
                part = part.reshape(256, depth)
                for h in range(1, depth // 128):
                    keep = part[:, :128] if h == 1 else keep
                    keep = jnp.where(half == h, part[:, 128 * h : 128 * h + 128], keep)
                part = keep if depth > 128 else part
                pick = jnp.where(wanted == column - 16 * k, 1.0, 0.0)
                pick = jnp.where(column // 16 == k, pick, 0.0).astype(BF16)
                total = total + lax.dot_general(
                    pick, part, (((1,), (1,)), ((), ())), preferred_element_type=F32
                )
            block_v[j] = total.astype(BF16)
            return carry

        lax.fori_loop(0, drops, extract, 0, unroll=4)

        for i in range(1, members):
            peer = lax.rem(member + members - i, members)
            pltpu.make_async_remote_copy(
                src_ref=pack_v.at[peer],
                dst_ref=got_v.at[peer],
                send_sem=send_sem.at[i],
                recv_sem=recv_sem.at[i],
                device_id=(group, peer),
                device_id_type=MESH,
            ).wait_recv()

        def pair_row(j, q):
            both = got_v[owner_s[j], q]
            return jnp.where(place_s[j] == 0, both[0:1], both[1:2])

        def sample(j, carry):
            row, deep = cell_parts(pair_row(j, 4))
            picked = jnp.dot(block_v[j], hot_rows(row), preferred_element_type=F32)
            hot = hot_depth(deep)
            for q in range(4):
                samp_v[j, q : q + 1] = jnp.sum(
                    picked[16 * q : 16 * q + 16] * hot, axis=0, keepdims=True
                )
            return carry

        lax.fori_loop(0, drops, sample, 0, unroll=4)
        samp_v[drops, 0:3] = jnp.zeros((3, parcels), F32)
        samp_v[drops, 3:4] = jnp.ones((1, parcels), F32)

        def give(s, carry):
            give_v[s // CAP, s % CAP] = samp_v[slot_s[s]].astype(BF16)
            return carry

        lax.fori_loop(0, members * CAP, give, 0, unroll=8)
        for i in range(1, members):
            peer = lax.rem(member + i, members)
            copy = pltpu.make_async_remote_copy(
                src_ref=give_v.at[peer],
                dst_ref=back_ref.at[member],
                send_sem=back_send.at[i],
                recv_sem=back_recv.at[i],
                device_id=(group, peer),
                device_id_type=MESH,
            )
            copy.start()
        back_ref[member] = give_v[member]

        def scatter(j, carry):
            row, deep = cell_parts(pair_row(j, 4))
            hot = hot_depth(deep)
            pull = pair_row(j, 3) * (1.0 - samp_v[j, 3:4])
            parts = []
            for q in range(3):
                drag = pull * (samp_v[j, q : q + 1] - pair_row(j, q))
                parts.append((drag.astype(BF16).astype(F32) * hot).astype(BF16))
            spread = jnp.concatenate(parts, axis=0)
            source = lax.dot_general(
                hot_rows(row), spread, (((1,), (1,)), ((), ())), preferred_element_type=F32
            )
            source_ref[j] = source.astype(BF16)
            return carry

        lax.fori_loop(0, drops, scatter, 0, unroll=4)

    edges(0)
    fluxx_v[...] = flux(vel_v[0, 0, 3].astype(F32), frac_v[0, 3], frac_v[0, 4])

    def plane(n, carry):
        @pl.when(jnp.logical_and(lax.rem(n, 4) == 2, n < quads - 4))
        def _():
            edges(lax.div(n, 4) + 1)

        @pl.when(n == quads - 6)
        def _():
            for copy in side_faces():
                copy.start()
            drag()

        @pl.when(n == quads - 2)
        def _():
            for copy in faces + side_faces():
                copy.wait()
            frac_v[blocks_x, 0] = hxn_v[...] * high_x

        @pl.when(n == quads - 1)
        def _():
            fluxx_v[...] = flux(hxu_v[...].astype(F32) * low_x, hxf_v[...], frac_v[0, 0])

        quad(lax.rem(n + 1, quads))
        return carry

    lax.fori_loop(0, quads, plane, 0)
    lax.fori_loop(0, blocks_x * 16, mend, 0, unroll=8)

    for i in range(1, members):
        peer = lax.rem(member + members - i, members)
        pltpu.make_async_remote_copy(
            src_ref=give_v.at[peer],
            dst_ref=back_ref.at[peer],
            send_sem=back_send.at[i],
            recv_sem=back_recv.at[i],
            device_id=(group, peer),
            device_id_type=MESH,
        ).wait()
    for copy in sends:
        copy.wait_send()


def field_kernel(
    block_s,
    vel_ref,
    next_ref,
    source_ref,
    back_ref,
    pv_ref,
    pr_ref,
    frac_out,
    vel_out,
    pv_out,
    fresh_v,
    lead_s,
    store_sem,
    block_sem,
):
    drops = block_s.shape[0]
    members = back_ref.shape[0]
    _, blocks_x, _, blocks_y, _, depth = vel_ref.shape
    blocks_z = depth // 16
    bulk = [
        pltpu.make_async_copy(vel_ref.at[:, c], vel_out.at[:, c], store_sem.at[c])
        for c in range(blocks_x)
    ]
    frac_copy = pltpu.make_async_copy(next_ref, frac_out, store_sem.at[blocks_x])
    for copy in bulk + [frac_copy]:
        copy.start()

    keys = [lax.div(block_s[j], 8) for j in range(drops)]
    for j in range(drops):
        lead = jnp.int32(j)
        for i in reversed(range(j)):
            lead = jnp.where(keys[i] == keys[j], i, lead)
        lead_s[j] = lead

    def spot(j):
        bx, by, bz = corner(block_s[j], blocks_y, blocks_z)
        z0 = pl.multiple_of(lax.div(bz, 8) * 128, 128)
        return bx, by, pl.ds(z0, 128), lax.rem(bz, 8) * 16

    def begin(j, carry):
        bx, by, lanes, _ = spot(j)
        for k in range(3):
            fresh_v[j, k] = vel_ref[k, bx, :, by, :, lanes]
        return carry

    lax.fori_loop(0, drops, begin, 0, unroll=4)

    lane = lax.broadcasted_iota(jnp.int32, (48, 128), 1)
    column = lax.broadcasted_iota(jnp.int32, (48, 128), 0)

    def patch(j, carry):
        _, _, _, shift = spot(j)
        wanted = lane - shift
        source = source_ref[j]
        lead = lead_s[j]
        for k in range(3):
            pick = jnp.where(wanted == column - 16 * k, 1.0, 0.0)
            pick = jnp.where(column // 16 == k, pick, 0.0).astype(BF16)
            moved = jnp.dot(source, pick, preferred_element_type=F32)
            old = fresh_v[lead, k].astype(F32).reshape(256, 128)
            fresh_v[lead, k] = (old + moved).astype(BF16).reshape(16, 16, 128)
        return carry

    lax.fori_loop(0, drops, patch, 0, unroll=4)

    def block_copy(j):
        bx, by, lanes, _ = spot(j)
        return pltpu.make_async_copy(
            fresh_v.at[j], vel_out.at[:, bx, :, by, :, lanes], block_sem.at[j]
        )

    for copy in bulk:
        copy.wait()
    for j in range(drops):

        @pl.when(lead_s[j] == j)
        def _():
            block_copy(j).start()

    def gain_pair(owner, carry):
        sampled = [back_ref[owner, place].astype(F32) for place in range(CAP)]
        rate = pr_ref[owner]
        old = pv_ref[owner]
        share = jnp.concatenate([s[3:4] for s in sampled], axis=0)
        pull = rate * (1.0 - share)
        for q in range(3):
            speed = jnp.concatenate([s[q : q + 1] for s in sampled], axis=0)
            pv_out[owner, q] = old[q] + pull * (speed - old[q])
        return carry

    lax.fori_loop(0, members, gain_pair, 0, unroll=4)
    frac_copy.wait()
    for j in range(drops):

        @pl.when(lead_s[j] == j)
        def _():
            block_copy(j).wait()


def solution(mesh):
    groups, members = mesh.shape["group"], mesh.shape["member"]

    def per_device(
        volume_frac,
        velocity,
        drop_block,
        drop_owner,
        parcel_vel,
        parcel_rate,
        parcel_weight,
        parcel_cell,
    ):
        planes, rows, depth = volume_frac.shape
        parcels = parcel_vel.shape[-1]
        drops = drop_block.shape[-1]
        block_ids = drop_block.reshape(drops)
        owners = drop_owner.reshape(drops)
        pv = parcel_vel[0, 0].transpose(0, 2, 1, 3)
        pr, pw, pc = parcel_rate[0, 0], parcel_weight[0, 0], parcel_cell[0, 0]
        smem = pl.BlockSpec(memory_space=pltpu.SMEM)
        vmem = pl.BlockSpec(memory_space=pltpu.VMEM)
        hbm = pl.BlockSpec(memory_space=pltpu.HBM)
        shaped = jax.ShapeDtypeStruct
        blocks_x, blocks_y = planes // 16, rows // 16
        vel6 = velocity.reshape(3, blocks_x, 16, blocks_y, 16, depth)
        frac5 = volume_frac.reshape(blocks_x, 16, blocks_y, 16, depth)
        face_x = (blocks_y, 16, depth)
        face_y = (blocks_x, 16, 1, depth)
        inputs = [
            pltpu.with_memory_space_constraint(a, pltpu.HBM)
            for a in (block_ids, owners, vel6, frac5, pv, pr, pw, pc)
        ]
        vel_now, frac_next, source, back = pl.pallas_call(
            functools.partial(exchange_kernel, groups, members),
            out_shape=(
                shaped(vel6.shape, BF16),
                shaped(frac5.shape, F32),
                shaped((drops, 256, 48), BF16),
                shaped((members, CAP, 4, parcels), BF16),
            ),
            in_specs=[hbm] * 8,
            out_specs=(vmem,) * 4,
            scratch_shapes=[
                pltpu.VMEM((blocks_x + 1, 16, blocks_y, 16, depth), F32),
                pltpu.VMEM(pv.shape, F32),
                pltpu.VMEM(pr.shape, F32),
                pltpu.VMEM(pw.shape, F32),
                pltpu.VMEM(pc.shape, jnp.int32),
                pltpu.VMEM((members, 5, CAP, parcels), F32),
                pltpu.VMEM((members, 5, CAP, parcels), F32),
                pltpu.VMEM((drops, 64, 256), BF16),
                pltpu.VMEM((drops + 1, 4, parcels), F32),
                pltpu.VMEM((members, CAP, 4, parcels), BF16),
                pltpu.VMEM(face_x, F32),
                pltpu.VMEM(face_x, BF16),
                pltpu.VMEM(face_x, F32),
                pltpu.VMEM(face_x, F32),
                pltpu.VMEM(face_y, F32),
                pltpu.VMEM(face_y, F32),
                pltpu.VMEM(face_y, F32),
                pltpu.VMEM(face_y, F32),
                pltpu.VMEM(face_y, F32),
                pltpu.VMEM(face_y, F32),
                pltpu.SMEM((drops,), jnp.int32),
                pltpu.SMEM((drops,), jnp.int32),
                pltpu.SMEM((drops,), jnp.int32),
                pltpu.SMEM((members * CAP,), jnp.int32),
                pltpu.SemaphoreType.DMA((2,)),
                pltpu.SemaphoreType.DMA((4,)),
                pltpu.SemaphoreType.DMA((2, blocks_x)),
                pltpu.SemaphoreType.DMA((members,)),
                pltpu.SemaphoreType.DMA((members,)),
                pltpu.SemaphoreType.DMA((members,)),
                pltpu.SemaphoreType.DMA((members,)),
                pltpu.SemaphoreType.DMA((6,)),
                pltpu.SemaphoreType.DMA((6,)),
            ],
            compiler_params=pltpu.CompilerParams(
                collective_id=0, has_side_effects=True, vmem_limit_bytes=40 << 20
            ),
            name="exchange",
        )(*inputs)
        frac_next, velocity_next, pv_next = pl.pallas_call(
            field_kernel,
            out_shape=(
                shaped(frac5.shape, F32),
                shaped(vel6.shape, BF16),
                shaped(pv.shape, F32),
            ),
            in_specs=[smem] + [vmem] * 6,
            out_specs=(hbm, hbm, vmem),
            scratch_shapes=[
                pltpu.VMEM((drops, 3, 16, 16, 128), BF16),
                pltpu.SMEM((drops,), jnp.int32),
                pltpu.SemaphoreType.DMA((blocks_x + 1,)),
                pltpu.SemaphoreType.DMA((drops,)),
            ],
            compiler_params=pltpu.CompilerParams(vmem_limit_bytes=40 << 20),
            name="field",
        )(block_ids, vel_now, frac_next, source, back, pv, pr)
        frac_next = frac_next.reshape(volume_frac.shape)
        velocity_next = velocity_next.reshape(velocity.shape)
        parcel_next = pv_next.transpose(0, 2, 1, 3)[None, None]
        return frac_next, velocity_next, parcel_next

    return jax.shard_map(
        per_device,
        mesh=mesh,
        in_specs=(
            P("group", "member", None),
            P(None, "group", "member", None),
            P("group", "member", None),
            P("group", "member", None, None),
            P("group", "member", None, None, None, None),
            P("group", "member", None, None, None),
            P("group", "member", None, None, None),
            P("group", "member", None, None, None),
        ),
        out_specs=(
            P("group", "member", None),
            P(None, "group", "member", None),
            P("group", "member", None, None, None, None),
        ),
        check_vma=False,
    )
```

```python
import functools

import jax
import jax.numpy as jnp
from jax import lax
from jax.experimental import pallas as pl
from jax.experimental.pallas import tpu as pltpu
from jax.sharding import PartitionSpec as P

CAP = 2
COURANT = 0.025
MESH = pl.DeviceIdType.MESH
F32 = jnp.float32
BF16 = jnp.bfloat16


def corner(block_id, blocks_y, blocks_z):
    first = lax.div(block_id, blocks_y * blocks_z)
    second = lax.rem(lax.div(block_id, blocks_z), blocks_y)
    third = lax.rem(block_id, blocks_z)
    return first, second, third


def cell_parts(cell):
    row = jnp.floor(cell * (1.0 / 16.0))
    return row, cell - 16.0 * row


def hot_rows(row):
    parcels = row.shape[-1]
    ids = lax.broadcasted_iota(jnp.int32, (256, parcels), 0).astype(F32)
    return jnp.where(ids == row, 1.0, 0.0).astype(BF16)


def hot_depth(depth):
    parcels = depth.shape[-1]
    ids = lax.broadcasted_iota(jnp.int32, (16, parcels), 0).astype(F32)
    return jnp.where(ids == depth, 1.0, 0.0)


def exchange_kernel(
    groups,
    members,
    block_hbm,
    owner_hbm,
    vel_hbm,
    frac_hbm,
    pv_hbm,
    pr_hbm,
    pw_hbm,
    pc_hbm,
    vel_v,
    next_v,
    source_ref,
    back_ref,
    frac_v,
    pv_v,
    pr_v,
    pw_v,
    pc_v,
    pack_v,
    got_v,
    block_v,
    samp_v,
    give_v,
    fluxx_v,
    hxu_v,
    hxf_v,
    hxn_v,
    hyu_v,
    hyf_v,
    hyn_v,
    syu_v,
    syf_v,
    syn_v,
    block_s,
    owner_s,
    place_s,
    slot_s,
    name_sem,
    parcel_sem,
    load_sem,
    send_sem,
    recv_sem,
    back_send,
    back_recv,
    face_send,
    face_recv,
):
    group = lax.axis_index("group")
    member = lax.axis_index("member")
    drops = owner_hbm.shape[0]
    blocks_x, _, blocks_y, _, depth = frac_hbm.shape
    parcels = pv_hbm.shape[-1]
    blocks_z = depth // 16

    parcel_loads = [
        pltpu.make_async_copy(src, dst, parcel_sem.at[i])
        for i, (src, dst) in enumerate(
            [(pv_hbm, pv_v), (pr_hbm, pr_v), (pw_hbm, pw_v), (pc_hbm, pc_v)]
        )
    ]
    def chunk_loads(c):
        return (
            pltpu.make_async_copy(frac_hbm.at[c], frac_v.at[c], load_sem.at[0, c]),
            pltpu.make_async_copy(vel_hbm.at[:, c], vel_v.at[:, c], load_sem.at[1, c]),
        )

    names = [
        pltpu.make_async_copy(block_hbm, block_s, name_sem.at[0]),
        pltpu.make_async_copy(owner_hbm, owner_s, name_sem.at[1]),
    ]
    for copy in names + parcel_loads:
        copy.start()
    for c in range(2):
        for copy in chunk_loads(c):
            copy.start()

    up = lax.rem(group + 1, groups)
    down = lax.rem(group + groups - 1, groups)
    right = lax.rem(member + 1, members)
    left = lax.rem(member + members - 1, members)
    barrier = pltpu.get_barrier_semaphore()
    for i in range(1, members):
        peer = lax.rem(member + i, members)
        pl.semaphore_signal(barrier, inc=1, device_id=(group, peer), device_id_type=MESH)
    for near in (up, down):
        pl.semaphore_signal(barrier, inc=1, device_id=(near, member), device_id_type=MESH)

    for copy in names:
        copy.wait()
    owners = [owner_s[j] for j in range(drops)]
    slots = []
    for j in range(drops):
        place = jnp.int32(0)
        for i in range(j):
            place = place + jnp.where(owners[i] == owners[j], 1, 0)
        place_s[j] = place
        slots.append(owners[j] * CAP + place)
    for s in range(members * CAP):
        found = jnp.int32(drops)
        for j in range(drops):
            found = jnp.where(slots[j] == s, j, found)
        slot_s[s] = found

    for copy in parcel_loads:
        copy.wait()
    pack_v[:, 0:3] = pv_v[...]
    pack_v[:, 3] = pr_v[...] * pw_v[...]
    pack_v[:, 4] = pc_v[...].astype(F32)

    low_x = jnp.where(group > 0, 1.0, 0.0)
    high_x = jnp.where(group < groups - 1, 1.0, 0.0)
    low_y = jnp.where(member > 0, 1.0, 0.0)
    high_y = jnp.where(member < members - 1, 1.0, 0.0)

    def flux(speed, here, there):
        return speed * jnp.where(speed > 0.0, here, there)

    row_id = lax.broadcasted_iota(jnp.int32, (8, 128), 0)
    lane_id = lax.broadcasted_iota(jnp.int32, (8, 128), 1)
    first_row, last_row = row_id == 0, row_id == 7
    first_lane, last_lane = lane_id == 0, lane_id == 127
    halves = [slice(h * 128, h * 128 + 128) for h in range(depth // 128)]
    tiles = blocks_y * 2
    nothing = jnp.zeros((8, 128), F32)

    def one_plane(bx, x):
        def at(t):
            return t // 2, slice(8 * (t % 2), 8 * (t % 2) + 8)

        def speeds(k, t):
            pairs = [vel_v[k, bx, x, t, :, h].astype(F32) for h in halves]
            return [[p[8 * i : 8 * i + 8] for p in pairs] for i in range(2)]

        after = bx * 16 + x + 1
        bn, xn = lax.div(after, 16), lax.rem(after, 16)
        here = [[frac_v[(bx, x) + at(t) + (h,)] for h in halves] for t in range(tiles)]
        behind = [nothing] * len(halves)
        rolled = [pltpu.roll(f, 7, 0) for f in here[0]]
        for t in range(tiles):
            if t % 2 == 0:
                pair = [speeds(k, t // 2) for k in range(3)]
            speed = [pair[k][t % 2] for k in range(3)]
            if t + 1 < tiles:
                rolled_next = [pltpu.roll(f, 7, 0) for f in here[t + 1]]
            else:
                rolled_next = [nothing] * len(halves)
            lanes = [pltpu.roll(f, 127, 1) for f in here[t]] + [nothing]
            deep = [
                flux(speed[2][i], here[t][i], jnp.where(last_lane, lanes[i + 1], lanes[i]))
                for i in range(len(halves))
            ]
            turned = [nothing] + [pltpu.roll(d, 1, 1) for d in deep]
            for i, h in enumerate(halves):
                spot = at(t) + (h,)
                now = flux(speed[0][i], here[t][i], frac_v[(bn, xn) + spot])
                change = now - fluxx_v[spot]
                fluxx_v[spot] = now
                ahead = jnp.where(last_row, rolled_next[i], rolled[i])
                now = flux(speed[1][i], here[t][i], ahead)
                moved = pltpu.roll(now, 1, 0)
                change = change + (now - jnp.where(first_row, behind[i], moved))
                behind[i] = moved
                under = jnp.where(first_lane, turned[i], turned[i + 1])
                change = change + (deep[i] - under)
                fresh = here[t][i] - COURANT * change
                capped = jnp.minimum(fresh, 1.0)
                if t == 0:
                    capped = jnp.where(first_row, fresh, capped)
                if t == tiles - 1:
                    capped = jnp.where(last_row, fresh, capped)
                next_v[(bx, x) + spot] = capped
            rolled = rolled_next

    quads = blocks_x * 4

    def quad(n):
        bx, x = lax.div(n, 4), lax.rem(n, 4) * 4
        for i in range(4):
            one_plane(bx, x + i)

    def mend(n, carry):
        bx, x = lax.div(n, 16), lax.rem(n, 16)
        gain = flux(hyu_v[bx, x] * low_y, hyf_v[bx, x], syn_v[bx, x])
        old = next_v[bx, x, 0, 0:1, :]
        next_v[bx, x, 0, 0:1, :] = jnp.minimum(old + COURANT * gain, 1.0)
        loss = jnp.minimum(syu_v[bx, x], 0.0) * (hyn_v[bx, x] * high_y)
        old = next_v[bx, x, blocks_y - 1, 15:16, :]
        next_v[bx, x, blocks_y - 1, 15:16, :] = jnp.minimum(old - COURANT * loss, 1.0)
        return carry

    def edges(c):
        for copy in chunk_loads(c):
            copy.wait()

        @pl.when(c + 2 < blocks_x)
        def _():
            for copy in chunk_loads(c + 2):
                copy.start()

        def edge(x, carry):
            syf_v[c, x] = frac_v[c, x, blocks_y - 1, 15:16, :]
            syn_v[c, x] = frac_v[c, x, 0, 0:1, :]
            syu_v[c, x] = vel_v[1, c, x, blocks_y - 1].astype(F32)[15:16]
            return carry

        lax.fori_loop(0, 16, edge, 0, unroll=8)

    def face(src, dst, number, device):
        copy = pltpu.make_async_remote_copy(
            src_ref=src,
            dst_ref=dst,
            send_sem=face_send.at[number],
            recv_sem=face_recv.at[number],
            device_id=device,
            device_id_type=MESH,
        )
        return copy

    def end_faces():
        return [
            face(vel_hbm.at[0, blocks_x - 1, 15], hxu_v, 0, (up, member)),
            face(frac_hbm.at[blocks_x - 1, 15], hxf_v, 1, (up, member)),
            face(frac_hbm.at[0, 0], hxn_v, 2, (down, member)),
        ]

    def send_out():
        pl.semaphore_wait(barrier, members + 1)

        for i in range(1, members):
            peer = lax.rem(member + i, members)
            copy = pltpu.make_async_remote_copy(
                src_ref=pack_v.at[peer],
                dst_ref=got_v.at[member],
                send_sem=send_sem.at[i],
                recv_sem=recv_sem.at[i],
                device_id=(group, peer),
                device_id_type=MESH,
            )
            copy.start()
        got_v[member] = pack_v[member]
        for copy in end_faces():
            copy.start()

    def side_faces():
        return [
            face(syu_v, hyu_v, 3, (group, right)),
            face(syf_v, hyf_v, 4, (group, right)),
            face(syn_v, hyn_v, 5, (group, left)),
        ]

    def drag():
        column = lax.broadcasted_iota(jnp.int32, (64, 128), 0)
        lane = lax.broadcasted_iota(jnp.int32, (64, 128), 1)

        def extract(j, carry):
            bx, by, bz = corner(block_s[j], blocks_y, blocks_z)
            half = lax.div(bz, 8)
            wanted = lane - lax.rem(bz, 8) * 16
            total = jnp.zeros((64, 256), F32)
            for k in range(4):
                if k < 3:
                    part = vel_v[k, bx, :, by]
                else:
                    part = frac_v[bx, :, by].astype(BF16)
                part = part.reshape(256, depth)
                for h in range(1, depth // 128):
                    keep = part[:, :128] if h == 1 else keep
                    keep = jnp.where(half == h, part[:, 128 * h : 128 * h + 128], keep)
                part = keep if depth > 128 else part
                pick = jnp.where(wanted == column - 16 * k, 1.0, 0.0)
                pick = jnp.where(column // 16 == k, pick, 0.0).astype(BF16)
                total = total + lax.dot_general(
                    pick, part, (((1,), (1,)), ((), ())), preferred_element_type=F32
                )
            block_v[j] = total.astype(BF16)
            return carry

        lax.fori_loop(0, drops, extract, 0, unroll=8)

        for i in range(1, members):
            peer = lax.rem(member + members - i, members)
            pltpu.make_async_remote_copy(
                src_ref=pack_v.at[peer],
                dst_ref=got_v.at[peer],
                send_sem=send_sem.at[i],
                recv_sem=recv_sem.at[i],
                device_id=(group, peer),
                device_id_type=MESH,
            ).wait()

        def pair_row(j, q):
            both = got_v[owner_s[j], q]
            return jnp.where(place_s[j] == 0, both[0:1], both[1:2])

        def sample(j, carry):
            row, deep = cell_parts(pair_row(j, 4))
            picked = jnp.dot(block_v[j], hot_rows(row), preferred_element_type=F32)
            hot = hot_depth(deep)
            for q in range(4):
                samp_v[j, q : q + 1] = jnp.sum(
                    picked[16 * q : 16 * q + 16] * hot, axis=0, keepdims=True
                )
            return carry

        lax.fori_loop(0, drops, sample, 0, unroll=8)
        samp_v[drops, 0:3] = jnp.zeros((3, parcels), F32)
        samp_v[drops, 3:4] = jnp.ones((1, parcels), F32)

        def give(s, carry):
            give_v[s // CAP, s % CAP] = samp_v[slot_s[s]].astype(BF16)
            return carry

        lax.fori_loop(0, members * CAP, give, 0, unroll=16)
        for i in range(1, members):
            peer = lax.rem(member + i, members)
            copy = pltpu.make_async_remote_copy(
                src_ref=give_v.at[peer],
                dst_ref=back_ref.at[member],
                send_sem=back_send.at[i],
                recv_sem=back_recv.at[i],
                device_id=(group, peer),
                device_id_type=MESH,
            )
            copy.start()
        back_ref[member] = give_v[member]

        def scatter(j, carry):
            row, deep = cell_parts(pair_row(j, 4))
            hot = hot_depth(deep)
            pull = pair_row(j, 3) * (1.0 - samp_v[j, 3:4])
            parts = []
            for q in range(3):
                drag = pull * (samp_v[j, q : q + 1] - pair_row(j, q))
                parts.append((drag.astype(BF16).astype(F32) * hot).astype(BF16))
            spread = jnp.concatenate(parts, axis=0)
            source = lax.dot_general(
                hot_rows(row), spread, (((1,), (1,)), ((), ())), preferred_element_type=F32
            )
            source_ref[j] = source.astype(BF16)
            return carry

        lax.fori_loop(0, drops, scatter, 0, unroll=8)

    send_out()

    edges(jnp.int32(0))
    fluxx_v[...] = flux(vel_v[0, 0, 3].astype(F32), frac_v[0, 3], frac_v[0, 4])

    def plane(n, carry):
        @pl.when(jnp.logical_and(lax.rem(n, 4) == 2, n < quads - 4))
        def _():
            edges(lax.div(n, 4) + 1)

        @pl.when(n == quads - 6)
        def _():
            for copy in side_faces():
                copy.start()

        @pl.when(n == quads - 6)
        def _():
            drag()

        @pl.when(n == quads - 2)
        def _():
            for copy in end_faces() + side_faces():
                copy.wait()
            frac_v[blocks_x, 0] = hxn_v[...] * high_x

        @pl.when(n == quads - 1)
        def _():
            fluxx_v[...] = flux(hxu_v[...].astype(F32) * low_x, hxf_v[...], frac_v[0, 0])

        quad(lax.rem(n + 1, quads))
        return carry

    lax.fori_loop(0, quads, plane, 0)
    lax.fori_loop(0, blocks_x * 16, mend, 0, unroll=16)

    for i in range(1, members):
        peer = lax.rem(member + members - i, members)
        pltpu.make_async_remote_copy(
            src_ref=give_v.at[peer],
            dst_ref=back_ref.at[peer],
            send_sem=back_send.at[i],
            recv_sem=back_recv.at[i],
            device_id=(group, peer),
            device_id_type=MESH,
        ).wait()


def field_kernel(
    block_s,
    vel_ref,
    next_ref,
    source_ref,
    back_ref,
    pv_ref,
    pr_ref,
    frac_out,
    vel_out,
    pv_out,
    fresh_v,
    pv_v,
    lead_s,
    store_sem,
    block_sem,
):
    drops = block_s.shape[0]
    members = back_ref.shape[0]
    _, blocks_x, _, blocks_y, _, depth = vel_ref.shape
    blocks_z = depth // 16
    bulk = [
        pltpu.make_async_copy(vel_ref.at[:, c], vel_out.at[:, c], store_sem.at[c])
        for c in range(blocks_x)
    ]
    frac_copy = pltpu.make_async_copy(next_ref, frac_out, store_sem.at[blocks_x])
    for copy in bulk:
        copy.start()

    def gain_pair(owner, carry):
        sampled = [back_ref[owner, place].astype(F32) for place in range(CAP)]
        rate = pr_ref[owner]
        old = pv_ref[owner]
        share = jnp.concatenate([s[3:4] for s in sampled], axis=0)
        pull = rate * (1.0 - share)
        for q in range(3):
            speed = jnp.concatenate([s[q : q + 1] for s in sampled], axis=0)
            pv_v[owner, q] = old[q] + pull * (speed - old[q])
        return carry

    lax.fori_loop(0, members, gain_pair, 0, unroll=4)
    pv_copy = pltpu.make_async_copy(pv_v, pv_out, store_sem.at[blocks_x + 1])
    pv_copy.start()

    keys = [lax.div(block_s[j], 8) for j in range(drops)]
    for j in range(drops):
        lead = jnp.int32(j)
        for i in reversed(range(j)):
            lead = jnp.where(keys[i] == keys[j], i, lead)
        lead_s[j] = lead

    def spot(j):
        bx, by, bz = corner(block_s[j], blocks_y, blocks_z)
        z0 = pl.multiple_of(lax.div(bz, 8) * 128, 128)
        return bx, by, pl.ds(z0, 128), lax.rem(bz, 8) * 16

    def begin(j, carry):
        bx, by, lanes, _ = spot(j)
        for k in range(3):
            fresh_v[j, k] = vel_ref[k, bx, :, by, :, lanes]
        return carry

    lax.fori_loop(0, drops, begin, 0, unroll=8)

    lane = lax.broadcasted_iota(jnp.int32, (48, 128), 1)
    column = lax.broadcasted_iota(jnp.int32, (48, 128), 0)

    def patch(j, carry):
        _, _, _, shift = spot(j)
        wanted = lane - shift
        source = source_ref[j]
        lead = lead_s[j]
        for k in range(3):
            pick = jnp.where(wanted == column - 16 * k, 1.0, 0.0)
            pick = jnp.where(column // 16 == k, pick, 0.0).astype(BF16)
            moved = jnp.dot(source, pick, preferred_element_type=F32)
            old = fresh_v[lead, k].astype(F32).reshape(256, 128)
            fresh_v[lead, k] = (old + moved).astype(BF16).reshape(16, 16, 128)
        return carry

    lax.fori_loop(0, drops, patch, 0, unroll=8)

    def block_copy(j):
        bx, by, lanes, _ = spot(j)
        return pltpu.make_async_copy(
            fresh_v.at[j], vel_out.at[:, bx, :, by, :, lanes], block_sem.at[j]
        )

    frac_copy.start()
    for copy in bulk:
        copy.wait()
    for j in range(drops):

        @pl.when(lead_s[j] == j)
        def _():
            block_copy(j).start()

    frac_copy.wait()
    pv_copy.wait()
    for j in range(drops):

        @pl.when(lead_s[j] == j)
        def _():
            block_copy(j).wait()


def solution(mesh):
    groups, members = mesh.shape["group"], mesh.shape["member"]

    def per_device(
        volume_frac,
        velocity,
        drop_block,
        drop_owner,
        parcel_vel,
        parcel_rate,
        parcel_weight,
        parcel_cell,
    ):
        planes, rows, depth = volume_frac.shape
        parcels = parcel_vel.shape[-1]
        drops = drop_block.shape[-1]
        block_ids = drop_block.reshape(drops)
        owners = drop_owner.reshape(drops)
        pv = parcel_vel[0, 0].transpose(0, 2, 1, 3)
        pr, pw, pc = parcel_rate[0, 0], parcel_weight[0, 0], parcel_cell[0, 0]
        smem = pl.BlockSpec(memory_space=pltpu.SMEM)
        vmem = pl.BlockSpec(memory_space=pltpu.VMEM)
        hbm = pl.BlockSpec(memory_space=pltpu.HBM)
        shaped = jax.ShapeDtypeStruct
        blocks_x, blocks_y = planes // 16, rows // 16
        vel6 = velocity.reshape(3, blocks_x, 16, blocks_y, 16, depth)
        frac5 = volume_frac.reshape(blocks_x, 16, blocks_y, 16, depth)
        face_x = (blocks_y, 16, depth)
        face_y = (blocks_x, 16, 1, depth)
        inputs = [
            pltpu.with_memory_space_constraint(a, pltpu.HBM)
            for a in (block_ids, owners, vel6, frac5, pv, pr, pw, pc)
        ]
        vel_now, frac_next, source, back = pl.pallas_call(
            functools.partial(exchange_kernel, groups, members),
            out_shape=(
                shaped(vel6.shape, BF16),
                shaped(frac5.shape, F32),
                shaped((drops, 256, 48), BF16),
                shaped((members, CAP, 4, parcels), BF16),
            ),
            in_specs=[hbm] * 8,
            out_specs=(vmem,) * 4,
            scratch_shapes=[
                pltpu.VMEM((blocks_x + 1, 16, blocks_y, 16, depth), F32),
                pltpu.VMEM(pv.shape, F32),
                pltpu.VMEM(pr.shape, F32),
                pltpu.VMEM(pw.shape, F32),
                pltpu.VMEM(pc.shape, jnp.int32),
                pltpu.VMEM((members, 5, CAP, parcels), F32),
                pltpu.VMEM((members, 5, CAP, parcels), F32),
                pltpu.VMEM((drops, 64, 256), BF16),
                pltpu.VMEM((drops + 1, 4, parcels), F32),
                pltpu.VMEM((members, CAP, 4, parcels), BF16),
                pltpu.VMEM(face_x, F32),
                pltpu.VMEM(face_x, BF16),
                pltpu.VMEM(face_x, F32),
                pltpu.VMEM(face_x, F32),
                pltpu.VMEM(face_y, F32),
                pltpu.VMEM(face_y, F32),
                pltpu.VMEM(face_y, F32),
                pltpu.VMEM(face_y, F32),
                pltpu.VMEM(face_y, F32),
                pltpu.VMEM(face_y, F32),
                pltpu.SMEM((drops,), jnp.int32),
                pltpu.SMEM((drops,), jnp.int32),
                pltpu.SMEM((drops,), jnp.int32),
                pltpu.SMEM((members * CAP,), jnp.int32),
                pltpu.SemaphoreType.DMA((2,)),
                pltpu.SemaphoreType.DMA((4,)),
                pltpu.SemaphoreType.DMA((2, blocks_x)),
                pltpu.SemaphoreType.DMA((members,)),
                pltpu.SemaphoreType.DMA((members,)),
                pltpu.SemaphoreType.DMA((members,)),
                pltpu.SemaphoreType.DMA((members,)),
                pltpu.SemaphoreType.DMA((6,)),
                pltpu.SemaphoreType.DMA((6,)),
            ],
            compiler_params=pltpu.CompilerParams(
                collective_id=0, has_side_effects=True, vmem_limit_bytes=40 << 20
            ),
            name="exchange",
        )(*inputs)
        frac_next, velocity_next, pv_next = pl.pallas_call(
            field_kernel,
            out_shape=(
                shaped(frac5.shape, F32),
                shaped(vel6.shape, BF16),
                shaped(pv.shape, F32),
            ),
            in_specs=[smem] + [vmem] * 6,
            out_specs=(hbm, hbm, hbm),
            scratch_shapes=[
                pltpu.VMEM((drops, 3, 16, 16, 128), BF16),
                pltpu.VMEM(pv.shape, F32),
                pltpu.SMEM((drops,), jnp.int32),
                pltpu.SemaphoreType.DMA((blocks_x + 2,)),
                pltpu.SemaphoreType.DMA((drops,)),
            ],
            compiler_params=pltpu.CompilerParams(vmem_limit_bytes=40 << 20),
            name="field",
        )(block_ids, vel_now, frac_next, source, back, pv, pr)
        frac_next = frac_next.reshape(volume_frac.shape)
        velocity_next = velocity_next.reshape(velocity.shape)
        parcel_next = pv_next.transpose(0, 2, 1, 3)[None, None]
        return frac_next, velocity_next, parcel_next

    return jax.shard_map(
        per_device,
        mesh=mesh,
        in_specs=(
            P("group", "member", None),
            P(None, "group", "member", None),
            P("group", "member", None),
            P("group", "member", None, None),
            P("group", "member", None, None, None, None),
            P("group", "member", None, None, None),
            P("group", "member", None, None, None),
            P("group", "member", None, None, None),
        ),
        out_specs=(
            P("group", "member", None),
            P(None, "group", "member", None),
            P("group", "member", None, None, None, None),
        ),
        check_vma=False,
    )
```

```python
import functools

import jax
import jax.numpy as jnp
from jax import lax
from jax.experimental import pallas as pl
from jax.experimental.pallas import tpu as pltpu
from jax.sharding import PartitionSpec as P

CAP = 2
COURANT = 0.025
MESH = pl.DeviceIdType.MESH
F32 = jnp.float32
BF16 = jnp.bfloat16


def corner(block_id, blocks_y, blocks_z):
    first = lax.div(block_id, blocks_y * blocks_z)
    second = lax.rem(lax.div(block_id, blocks_z), blocks_y)
    third = lax.rem(block_id, blocks_z)
    return first, second, third


def cell_parts(cell):
    row = jnp.floor(cell * (1.0 / 16.0))
    return row, cell - 16.0 * row


def hot_rows(row):
    parcels = row.shape[-1]
    ids = lax.broadcasted_iota(jnp.int32, (256, parcels), 0).astype(F32)
    return jnp.where(ids == row, 1.0, 0.0).astype(BF16)


def hot_depth(depth):
    parcels = depth.shape[-1]
    ids = lax.broadcasted_iota(jnp.int32, (16, parcels), 0).astype(F32)
    return jnp.where(ids == depth, 1.0, 0.0)


def exchange_kernel(
    groups,
    members,
    block_hbm,
    owner_hbm,
    vel_hbm,
    frac_hbm,
    pv_hbm,
    pr_hbm,
    pw_hbm,
    pc_hbm,
    vel_v,
    next_v,
    source_ref,
    back_ref,
    frac_v,
    pv_v,
    pr_v,
    pw_v,
    pc_v,
    pack_v,
    got_v,
    block_v,
    samp_v,
    give_v,
    fluxx_v,
    hxu_v,
    hxf_v,
    hxn_v,
    hyu_v,
    hyf_v,
    hyn_v,
    syu_v,
    syf_v,
    syn_v,
    block_s,
    owner_s,
    place_s,
    slot_s,
    name_sem,
    parcel_sem,
    load_sem,
    send_sem,
    recv_sem,
    back_send,
    back_recv,
    face_send,
    face_recv,
):
    group = lax.axis_index("group")
    member = lax.axis_index("member")
    drops = owner_hbm.shape[0]
    blocks_x, _, blocks_y, _, depth = frac_hbm.shape
    parcels = pv_hbm.shape[-1]
    blocks_z = depth // 16

    parcel_loads = [
        pltpu.make_async_copy(src, dst, parcel_sem.at[i])
        for i, (src, dst) in enumerate(
            [(pv_hbm, pv_v), (pr_hbm, pr_v), (pw_hbm, pw_v), (pc_hbm, pc_v)]
        )
    ]
    def chunk_loads(c):
        return (
            pltpu.make_async_copy(frac_hbm.at[c], frac_v.at[c], load_sem.at[0, c]),
            pltpu.make_async_copy(vel_hbm.at[:, c], vel_v.at[:, c], load_sem.at[1, c]),
        )

    names = [
        pltpu.make_async_copy(block_hbm, block_s, name_sem.at[0]),
        pltpu.make_async_copy(owner_hbm, owner_s, name_sem.at[1]),
    ]
    for copy in names + parcel_loads:
        copy.start()
    for c in range(2):
        for copy in chunk_loads(c):
            copy.start()

    up = lax.rem(group + 1, groups)
    down = lax.rem(group + groups - 1, groups)
    right = lax.rem(member + 1, members)
    left = lax.rem(member + members - 1, members)
    barrier = pltpu.get_barrier_semaphore()
    for i in range(1, members):
        peer = lax.rem(member + i, members)
        pl.semaphore_signal(barrier, inc=1, device_id=(group, peer), device_id_type=MESH)
    for near in (up, down):
        pl.semaphore_signal(barrier, inc=1, device_id=(near, member), device_id_type=MESH)

    for copy in names:
        copy.wait()
    owners = [owner_s[j] for j in range(drops)]
    slots = []
    for j in range(drops):
        place = jnp.int32(0)
        for i in range(j):
            place = place + jnp.where(owners[i] == owners[j], 1, 0)
        place_s[j] = place
        slots.append(owners[j] * CAP + place)
    for s in range(members * CAP):
        found = jnp.int32(drops)
        for j in range(drops):
            found = jnp.where(slots[j] == s, j, found)
        slot_s[s] = found

    for copy in parcel_loads:
        copy.wait()
    pack_v[:, 0:3] = pv_v[...]
    pack_v[:, 3] = pr_v[...] * pw_v[...]
    pack_v[:, 4] = pc_v[...].astype(F32)

    low_x = jnp.where(group > 0, 1.0, 0.0)
    high_x = jnp.where(group < groups - 1, 1.0, 0.0)
    low_y = jnp.where(member > 0, 1.0, 0.0)
    high_y = jnp.where(member < members - 1, 1.0, 0.0)

    def flux(speed, here, there):
        return speed * jnp.where(speed > 0.0, here, there)

    row_id = lax.broadcasted_iota(jnp.int32, (8, 128), 0)
    lane_id = lax.broadcasted_iota(jnp.int32, (8, 128), 1)
    first_row, last_row = row_id == 0, row_id == 7
    first_lane, last_lane = lane_id == 0, lane_id == 127
    halves = [slice(h * 128, h * 128 + 128) for h in range(depth // 128)]
    tiles = blocks_y * 2
    nothing = jnp.zeros((8, 128), F32)

    def one_plane(bx, x):
        def at(t):
            return t // 2, slice(8 * (t % 2), 8 * (t % 2) + 8)

        def speeds(k, t):
            pairs = [vel_v[k, bx, x, t, :, h].astype(F32) for h in halves]
            return [[p[8 * i : 8 * i + 8] for p in pairs] for i in range(2)]

        after = bx * 16 + x + 1
        bn, xn = lax.div(after, 16), lax.rem(after, 16)
        here = [[frac_v[(bx, x) + at(t) + (h,)] for h in halves] for t in range(tiles)]
        behind = [nothing] * len(halves)
        rolled = [pltpu.roll(f, 7, 0) for f in here[0]]
        for t in range(tiles):
            if t % 2 == 0:
                pair = [speeds(k, t // 2) for k in range(3)]
            speed = [pair[k][t % 2] for k in range(3)]
            if t + 1 < tiles:
                rolled_next = [pltpu.roll(f, 7, 0) for f in here[t + 1]]
            else:
                rolled_next = [nothing] * len(halves)
            lanes = [pltpu.roll(f, 127, 1) for f in here[t]] + [nothing]
            deep = [
                flux(speed[2][i], here[t][i], jnp.where(last_lane, lanes[i + 1], lanes[i]))
                for i in range(len(halves))
            ]
            turned = [nothing] + [pltpu.roll(d, 1, 1) for d in deep]
            for i, h in enumerate(halves):
                spot = at(t) + (h,)
                now = flux(speed[0][i], here[t][i], frac_v[(bn, xn) + spot])
                change = now - fluxx_v[spot]
                fluxx_v[spot] = now
                ahead = jnp.where(last_row, rolled_next[i], rolled[i])
                now = flux(speed[1][i], here[t][i], ahead)
                moved = pltpu.roll(now, 1, 0)
                change = change + (now - jnp.where(first_row, behind[i], moved))
                behind[i] = moved
                under = jnp.where(first_lane, turned[i], turned[i + 1])
                change = change + (deep[i] - under)
                fresh = here[t][i] - COURANT * change
                capped = jnp.minimum(fresh, 1.0)
                if t == 0:
                    capped = jnp.where(first_row, fresh, capped)
                if t == tiles - 1:
                    capped = jnp.where(last_row, fresh, capped)
                next_v[(bx, x) + spot] = capped
            rolled = rolled_next

    quads = blocks_x * 4

    def quad(n):
        bx, x = lax.div(n, 4), lax.rem(n, 4) * 4
        for i in range(4):
            one_plane(bx, x + i)

    def mend(n, carry):
        bx, x = lax.div(n, 16), lax.rem(n, 16)
        gain = flux(hyu_v[bx, x] * low_y, hyf_v[bx, x], syn_v[bx, x])
        old = next_v[bx, x, 0, 0:1, :]
        next_v[bx, x, 0, 0:1, :] = jnp.minimum(old + COURANT * gain, 1.0)
        loss = jnp.minimum(syu_v[bx, x], 0.0) * (hyn_v[bx, x] * high_y)
        old = next_v[bx, x, blocks_y - 1, 15:16, :]
        next_v[bx, x, blocks_y - 1, 15:16, :] = jnp.minimum(old - COURANT * loss, 1.0)
        return carry

    def edges(c):
        for copy in chunk_loads(c):
            copy.wait()

        @pl.when(c + 2 < blocks_x)
        def _():
            for copy in chunk_loads(c + 2):
                copy.start()

        def edge(x, carry):
            syf_v[c, x] = frac_v[c, x, blocks_y - 1, 15:16, :]
            syn_v[c, x] = frac_v[c, x, 0, 0:1, :]
            syu_v[c, x] = vel_v[1, c, x, blocks_y - 1].astype(F32)[15:16]
            return carry

        lax.fori_loop(0, 16, edge, 0, unroll=8)

    def face(src, dst, number, device):
        copy = pltpu.make_async_remote_copy(
            src_ref=src,
            dst_ref=dst,
            send_sem=face_send.at[number],
            recv_sem=face_recv.at[number],
            device_id=device,
            device_id_type=MESH,
        )
        return copy

    def end_faces():
        return [
            face(vel_hbm.at[0, blocks_x - 1, 15], hxu_v, 0, (up, member)),
            face(frac_hbm.at[blocks_x - 1, 15], hxf_v, 1, (up, member)),
            face(frac_hbm.at[0, 0], hxn_v, 2, (down, member)),
        ]

    def send_out():
        pl.semaphore_wait(barrier, members + 1)

        for i in range(1, members):
            peer = lax.rem(member + i, members)
            copy = pltpu.make_async_remote_copy(
                src_ref=pack_v.at[peer],
                dst_ref=got_v.at[member],
                send_sem=send_sem.at[i],
                recv_sem=recv_sem.at[i],
                device_id=(group, peer),
                device_id_type=MESH,
            )
            copy.start()
        got_v[member] = pack_v[member]
        for copy in end_faces():
            copy.start()

    def side_faces():
        return [
            face(syu_v, hyu_v, 3, (group, right)),
            face(syf_v, hyf_v, 4, (group, right)),
            face(syn_v, hyn_v, 5, (group, left)),
        ]

    def collect():
        column = lax.broadcasted_iota(jnp.int32, (64, 128), 0)
        lane = lax.broadcasted_iota(jnp.int32, (64, 128), 1)

        def extract(j, carry):
            bx, by, bz = corner(block_s[j], blocks_y, blocks_z)
            half = lax.div(bz, 8)
            wanted = lane - lax.rem(bz, 8) * 16
            total = jnp.zeros((64, 256), F32)
            for k in range(4):
                if k < 3:
                    part = vel_v[k, bx, :, by]
                else:
                    part = frac_v[bx, :, by].astype(BF16)
                part = part.reshape(256, depth)
                for h in range(1, depth // 128):
                    keep = part[:, :128] if h == 1 else keep
                    keep = jnp.where(half == h, part[:, 128 * h : 128 * h + 128], keep)
                part = keep if depth > 128 else part
                pick = jnp.where(wanted == column - 16 * k, 1.0, 0.0)
                pick = jnp.where(column // 16 == k, pick, 0.0).astype(BF16)
                total = total + lax.dot_general(
                    pick, part, (((1,), (1,)), ((), ())), preferred_element_type=F32
                )
            block_v[j] = total.astype(BF16)
            return carry

        lax.fori_loop(0, drops, extract, 0, unroll=8)

    def drag():

        for i in range(1, members):
            peer = lax.rem(member + members - i, members)
            pltpu.make_async_remote_copy(
                src_ref=pack_v.at[peer],
                dst_ref=got_v.at[peer],
                send_sem=send_sem.at[i],
                recv_sem=recv_sem.at[i],
                device_id=(group, peer),
                device_id_type=MESH,
            ).wait()

        def pair_row(j, q):
            both = got_v[owner_s[j], q]
            return jnp.where(place_s[j] == 0, both[0:1], both[1:2])

        def sample(j, carry):
            row, deep = cell_parts(pair_row(j, 4))
            picked = jnp.dot(block_v[j], hot_rows(row), preferred_element_type=F32)
            hot = hot_depth(deep)
            for q in range(4):
                samp_v[j, q : q + 1] = jnp.sum(
                    picked[16 * q : 16 * q + 16] * hot, axis=0, keepdims=True
                )
            return carry

        lax.fori_loop(0, drops, sample, 0, unroll=8)
        samp_v[drops, 0:3] = jnp.zeros((3, parcels), F32)
        samp_v[drops, 3:4] = jnp.ones((1, parcels), F32)

        def give(s, carry):
            give_v[s // CAP, s % CAP] = samp_v[slot_s[s]].astype(BF16)
            return carry

        lax.fori_loop(0, members * CAP, give, 0, unroll=16)
        for i in range(1, members):
            peer = lax.rem(member + i, members)
            copy = pltpu.make_async_remote_copy(
                src_ref=give_v.at[peer],
                dst_ref=back_ref.at[member],
                send_sem=back_send.at[i],
                recv_sem=back_recv.at[i],
                device_id=(group, peer),
                device_id_type=MESH,
            )
            copy.start()
        back_ref[member] = give_v[member]

        def scatter(j, carry):
            row, deep = cell_parts(pair_row(j, 4))
            hot = hot_depth(deep)
            pull = pair_row(j, 3) * (1.0 - samp_v[j, 3:4])
            parts = []
            for q in range(3):
                drag = pull * (samp_v[j, q : q + 1] - pair_row(j, q))
                parts.append((drag.astype(BF16).astype(F32) * hot).astype(BF16))
            spread = jnp.concatenate(parts, axis=0)
            source = lax.dot_general(
                hot_rows(row), spread, (((1,), (1,)), ((), ())), preferred_element_type=F32
            )
            source_ref[j] = source.astype(BF16)
            return carry

        lax.fori_loop(0, drops, scatter, 0, unroll=8)

    send_out()

    edges(jnp.int32(0))
    fluxx_v[...] = flux(vel_v[0, 0, 3].astype(F32), frac_v[0, 3], frac_v[0, 4])

    def plane(n, carry):
        @pl.when(jnp.logical_and(lax.rem(n, 4) == 2, n < quads - 4))
        def _():
            edges(lax.div(n, 4) + 1)

        @pl.when(n == quads - 6)
        def _():
            for copy in side_faces():
                copy.start()

        @pl.when(n == quads - 6)
        def _():
            collect()

        @pl.when(n == quads - 4)
        def _():
            drag()

        @pl.when(n == quads - 2)
        def _():
            for copy in end_faces() + side_faces():
                copy.wait()
            frac_v[blocks_x, 0] = hxn_v[...] * high_x

        @pl.when(n == quads - 1)
        def _():
            fluxx_v[...] = flux(hxu_v[...].astype(F32) * low_x, hxf_v[...], frac_v[0, 0])

        quad(lax.rem(n + 1, quads))
        return carry

    lax.fori_loop(0, quads, plane, 0)
    lax.fori_loop(0, blocks_x * 16, mend, 0, unroll=16)

    for i in range(1, members):
        peer = lax.rem(member + members - i, members)
        pltpu.make_async_remote_copy(
            src_ref=give_v.at[peer],
            dst_ref=back_ref.at[peer],
            send_sem=back_send.at[i],
            recv_sem=back_recv.at[i],
            device_id=(group, peer),
            device_id_type=MESH,
        ).wait()


def field_kernel(
    block_s,
    vel_ref,
    next_ref,
    source_ref,
    back_ref,
    pv_ref,
    pr_ref,
    frac_out,
    vel_out,
    pv_out,
    fresh_v,
    pv_v,
    lead_s,
    store_sem,
    block_sem,
):
    drops = block_s.shape[0]
    members = back_ref.shape[0]
    _, blocks_x, _, blocks_y, _, depth = vel_ref.shape
    blocks_z = depth // 16
    bulk = [
        pltpu.make_async_copy(vel_ref.at[:, c], vel_out.at[:, c], store_sem.at[c])
        for c in range(blocks_x)
    ]
    frac_copy = pltpu.make_async_copy(next_ref, frac_out, store_sem.at[blocks_x])
    for copy in bulk:
        copy.start()

    def gain_pair(owner, carry):
        sampled = [back_ref[owner, place].astype(F32) for place in range(CAP)]
        rate = pr_ref[owner]
        old = pv_ref[owner]
        share = jnp.concatenate([s[3:4] for s in sampled], axis=0)
        pull = rate * (1.0 - share)
        for q in range(3):
            speed = jnp.concatenate([s[q : q + 1] for s in sampled], axis=0)
            pv_v[owner, q] = old[q] + pull * (speed - old[q])
        return carry

    lax.fori_loop(0, members, gain_pair, 0, unroll=4)
    pv_copy = pltpu.make_async_copy(pv_v, pv_out, store_sem.at[blocks_x + 1])
    pv_copy.start()

    keys = [lax.div(block_s[j], 8) for j in range(drops)]
    for j in range(drops):
        lead = jnp.int32(j)
        for i in reversed(range(j)):
            lead = jnp.where(keys[i] == keys[j], i, lead)
        lead_s[j] = lead

    def spot(j):
        bx, by, bz = corner(block_s[j], blocks_y, blocks_z)
        z0 = pl.multiple_of(lax.div(bz, 8) * 128, 128)
        return bx, by, pl.ds(z0, 128), lax.rem(bz, 8) * 16

    def begin(j, carry):
        bx, by, lanes, _ = spot(j)
        for k in range(3):
            fresh_v[j, k] = vel_ref[k, bx, :, by, :, lanes]
        return carry

    lax.fori_loop(0, drops, begin, 0, unroll=8)

    lane = lax.broadcasted_iota(jnp.int32, (48, 128), 1)
    column = lax.broadcasted_iota(jnp.int32, (48, 128), 0)

    def patch(j, carry):
        _, _, _, shift = spot(j)
        wanted = lane - shift
        source = source_ref[j]
        lead = lead_s[j]
        for k in range(3):
            pick = jnp.where(wanted == column - 16 * k, 1.0, 0.0)
            pick = jnp.where(column // 16 == k, pick, 0.0).astype(BF16)
            moved = jnp.dot(source, pick, preferred_element_type=F32)
            old = fresh_v[lead, k].astype(F32).reshape(256, 128)
            fresh_v[lead, k] = (old + moved).astype(BF16).reshape(16, 16, 128)
        return carry

    lax.fori_loop(0, drops, patch, 0, unroll=8)

    def block_copy(j):
        bx, by, lanes, _ = spot(j)
        return pltpu.make_async_copy(
            fresh_v.at[j], vel_out.at[:, bx, :, by, :, lanes], block_sem.at[j]
        )

    frac_copy.start()
    for copy in bulk:
        copy.wait()
    for j in range(drops):

        @pl.when(lead_s[j] == j)
        def _():
            block_copy(j).start()

    frac_copy.wait()
    pv_copy.wait()
    for j in range(drops):

        @pl.when(lead_s[j] == j)
        def _():
            block_copy(j).wait()


def solution(mesh):
    groups, members = mesh.shape["group"], mesh.shape["member"]

    def per_device(
        volume_frac,
        velocity,
        drop_block,
        drop_owner,
        parcel_vel,
        parcel_rate,
        parcel_weight,
        parcel_cell,
    ):
        planes, rows, depth = volume_frac.shape
        parcels = parcel_vel.shape[-1]
        drops = drop_block.shape[-1]
        block_ids = drop_block.reshape(drops)
        owners = drop_owner.reshape(drops)
        pv = parcel_vel[0, 0].transpose(0, 2, 1, 3)
        pr, pw, pc = parcel_rate[0, 0], parcel_weight[0, 0], parcel_cell[0, 0]
        smem = pl.BlockSpec(memory_space=pltpu.SMEM)
        vmem = pl.BlockSpec(memory_space=pltpu.VMEM)
        hbm = pl.BlockSpec(memory_space=pltpu.HBM)
        shaped = jax.ShapeDtypeStruct
        blocks_x, blocks_y = planes // 16, rows // 16
        vel6 = velocity.reshape(3, blocks_x, 16, blocks_y, 16, depth)
        frac5 = volume_frac.reshape(blocks_x, 16, blocks_y, 16, depth)
        face_x = (blocks_y, 16, depth)
        face_y = (blocks_x, 16, 1, depth)
        inputs = [
            pltpu.with_memory_space_constraint(a, pltpu.HBM)
            for a in (block_ids, owners, vel6, frac5, pv, pr, pw, pc)
        ]
        vel_now, frac_next, source, back = pl.pallas_call(
            functools.partial(exchange_kernel, groups, members),
            out_shape=(
                shaped(vel6.shape, BF16),
                shaped(frac5.shape, F32),
                shaped((drops, 256, 48), BF16),
                shaped((members, CAP, 4, parcels), BF16),
            ),
            in_specs=[hbm] * 8,
            out_specs=(vmem,) * 4,
            scratch_shapes=[
                pltpu.VMEM((blocks_x + 1, 16, blocks_y, 16, depth), F32),
                pltpu.VMEM(pv.shape, F32),
                pltpu.VMEM(pr.shape, F32),
                pltpu.VMEM(pw.shape, F32),
                pltpu.VMEM(pc.shape, jnp.int32),
                pltpu.VMEM((members, 5, CAP, parcels), F32),
                pltpu.VMEM((members, 5, CAP, parcels), F32),
                pltpu.VMEM((drops, 64, 256), BF16),
                pltpu.VMEM((drops + 1, 4, parcels), F32),
                pltpu.VMEM((members, CAP, 4, parcels), BF16),
                pltpu.VMEM(face_x, F32),
                pltpu.VMEM(face_x, BF16),
                pltpu.VMEM(face_x, F32),
                pltpu.VMEM(face_x, F32),
                pltpu.VMEM(face_y, F32),
                pltpu.VMEM(face_y, F32),
                pltpu.VMEM(face_y, F32),
                pltpu.VMEM(face_y, F32),
                pltpu.VMEM(face_y, F32),
                pltpu.VMEM(face_y, F32),
                pltpu.SMEM((drops,), jnp.int32),
                pltpu.SMEM((drops,), jnp.int32),
                pltpu.SMEM((drops,), jnp.int32),
                pltpu.SMEM((members * CAP,), jnp.int32),
                pltpu.SemaphoreType.DMA((2,)),
                pltpu.SemaphoreType.DMA((4,)),
                pltpu.SemaphoreType.DMA((2, blocks_x)),
                pltpu.SemaphoreType.DMA((members,)),
                pltpu.SemaphoreType.DMA((members,)),
                pltpu.SemaphoreType.DMA((members,)),
                pltpu.SemaphoreType.DMA((members,)),
                pltpu.SemaphoreType.DMA((6,)),
                pltpu.SemaphoreType.DMA((6,)),
            ],
            compiler_params=pltpu.CompilerParams(
                collective_id=0, has_side_effects=True, vmem_limit_bytes=40 << 20
            ),
            name="exchange",
        )(*inputs)
        frac_next, velocity_next, pv_next = pl.pallas_call(
            field_kernel,
            out_shape=(
                shaped(frac5.shape, F32),
                shaped(vel6.shape, BF16),
                shaped(pv.shape, F32),
            ),
            in_specs=[smem] + [vmem] * 6,
            out_specs=(hbm, hbm, hbm),
            scratch_shapes=[
                pltpu.VMEM((drops, 3, 16, 16, 128), BF16),
                pltpu.VMEM(pv.shape, F32),
                pltpu.SMEM((drops,), jnp.int32),
                pltpu.SemaphoreType.DMA((blocks_x + 2,)),
                pltpu.SemaphoreType.DMA((drops,)),
            ],
            compiler_params=pltpu.CompilerParams(vmem_limit_bytes=40 << 20),
            name="field",
        )(block_ids, vel_now, frac_next, source, back, pv, pr)
        frac_next = frac_next.reshape(volume_frac.shape)
        velocity_next = velocity_next.reshape(velocity.shape)
        parcel_next = pv_next.transpose(0, 2, 1, 3)[None, None]
        return frac_next, velocity_next, parcel_next

    return jax.shard_map(
        per_device,
        mesh=mesh,
        in_specs=(
            P("group", "member", None),
            P(None, "group", "member", None),
            P("group", "member", None),
            P("group", "member", None, None),
            P("group", "member", None, None, None, None),
            P("group", "member", None, None, None),
            P("group", "member", None, None, None),
            P("group", "member", None, None, None),
        ),
        out_specs=(
            P("group", "member", None),
            P(None, "group", "member", None),
            P("group", "member", None, None, None, None),
        ),
        check_vma=False,
    )
```
